256 devices in a mesh: ka: 32 (over x, z_lo, core), tr: 2 (over z_hi), tc: 4 (over y).
Axes of the slice: x: 4, y: 4, z: 8 (z_hi: 2, z_lo: 4; z = z_hi * 4 + z_lo), core: 2. Of those that a mesh axis runs over, the one named last changes fastest.
Arguments:
- green_less: float32 [2, 32, 1024, 1024], P(None, 'ka', 'tr', 'tc'), may hold values from -6 to 6
- green_great: float32 [2, 32, 1024, 1024], P(None, 'ka', 'tr', 'tc'), may hold values from -6 to 6
- screened: float32 [2, 32, 1024, 1024], P(None, 'ka', 'tr', 'tc'), may hold values from -6 to 6
Outputs:
- collision: float32 [2, 32, 1024, 1024], P(None, 'ka', 'tr', 'tc')
- green_next: float32 [2, 32, 1024, 1024], P(None, 'ka', 'tr', 'tc')
The draws below stay inside these ranges and needn't reach their ends.
All inputs are finite; a program needn't handle non-finite values.
Results may differ from the reference program's by a relative error of at most 0.00012.
Values sent between devices are 32-bit elements; how exact they have to be, the bound alone decides.
A program may use at most 64 MiB of HBM per device.

```python
import math
import jax
import jax.numpy as jnp
from jax import lax

K = 32
NT = 1024


def block_levels(rng, extent, split, smallest, largest):
    factor_of, own = 1.0, jax.random.fold_in(rng, 6)
    for axis_at, shards_of in split:
        draws = jnp.exp(jax.random.uniform(jax.random.fold_in(own, axis_at), (shards_of,), jnp.float32, smallest / len(split), largest / len(split)))
        factor_of = factor_of * jnp.repeat(draws, extent[axis_at] // shards_of).reshape([-1 if axis == axis_at else 1 for axis in range(len(extent))])
    return factor_of


def normal_values(rng, extent, spread, reach, split=(), kind=jnp.bfloat16):
    result = jax.random.normal(rng, extent, jnp.float32) * spread
    if len(split) > 0:
        result = block_levels(rng, extent, split, -0.22, 0.18) * result
    return jnp.clip(result, min=-reach, max=reach).astype(kind)


def setup_inputs(seed: int = 0) -> dict:
    seeds = jax.random.split(jax.random.key(seed), 4)
    green_less = normal_values(seeds[0], (2, K, NT, NT), 1.0, 6.0, ((1, 32), (2, 2), (3, 4)), jnp.float32)
    green_great = normal_values(seeds[1], (2, K, NT, NT), 1.0, 6.0, ((1, 32), (2, 2), (3, 4)), jnp.float32)
    screened = normal_values(seeds[2], (2, K, NT, NT), 1.0, 6.0, ((1, 32), (2, 2), (3, 4)), jnp.float32)
    return {"green_less": green_less, "green_great": green_great, "screened": screened}


def angle_tables(points):
    indices = jnp.arange(points, dtype=jnp.int32)
    phases = (indices[:, None] * indices[None, :]) % points
    angles = phases.astype(jnp.float32) * (2.0 * math.pi / points)
    return jnp.cos(angles), jnp.sin(angles)


def along_momenta(matrix_in, source):
    return jnp.tensordot(matrix_in, source, axes=1, precision=lax.Precision.HIGHEST)


def to_real(source, cosine_table, sine_table):
    factor = source.shape[1] ** -0.5
    real_part = along_momenta(cosine_table, source[0]) - along_momenta(sine_table, source[1])
    imag_part = along_momenta(cosine_table, source[1]) + along_momenta(sine_table, source[0])
    return jnp.stack([real_part, imag_part]) * factor


def to_momentum(source, cosine_table, sine_table):
    factor = source.shape[1] ** -0.5
    real_part = along_momenta(cosine_table, source[0]) + along_momenta(sine_table, source[1])
    imag_part = along_momenta(cosine_table, source[1]) - along_momenta(sine_table, source[0])
    return jnp.stack([real_part, imag_part]) * factor


def self_energy(less_tiles, great_tiles, screen_tiles, cosine_table, sine_table):
    lesser = to_real(less_tiles, cosine_table, sine_table)
    greater = to_real(great_tiles, cosine_table, sine_table)
    screen_real = to_real(screen_tiles, cosine_table, sine_table)
    polar_real = lesser[0] * greater[1] - lesser[1] * greater[0]
    polar_imag = lesser[0] * greater[0] + lesser[1] * greater[1]
    inter_real = screen_real[0] + polar_real
    inter_imag = screen_real[1] + polar_imag
    sigma_re = -(lesser[0] * inter_imag + lesser[1] * inter_real)
    sigma_im = lesser[0] * inter_real - lesser[1] * inter_imag
    return to_momentum(jnp.stack([sigma_re, sigma_im]), cosine_table, sine_table)


def matrix_product(left, right):
    return jnp.dot(left, right, preferred_element_type=jnp.float32, precision=lax.Precision.HIGHEST)


def reference(green_less, green_great, screened):
    points = green_less.shape[1]
    length = green_less.shape[2]
    blocks = length // 128
    cosine_table, sine_table = angle_tables(points)

    def split_rows(source):
        return jnp.moveaxis(source.reshape(2, points, blocks, 128, length), 2, 0)

    def one_block(pieces):
        return self_energy(pieces[0], pieces[1], pieces[2], cosine_table, sine_table)

    sigma_blocks = lax.map(one_block, (split_rows(green_less), split_rows(green_great), split_rows(screened)))
    sigma_tiles = jnp.moveaxis(sigma_blocks, 0, 2).reshape(2, points, length, length)

    def one_momentum(pieces):
        left_side, right_side = pieces
        real_part = matrix_product(left_side[0], right_side[0]) - matrix_product(left_side[1], right_side[1])
        imag_part = matrix_product(left_side[0], right_side[1]) + matrix_product(left_side[1], right_side[0])
        return jnp.stack([real_part, imag_part])

    products = lax.map(one_momentum, (jnp.moveaxis(sigma_tiles, 1, 0), jnp.moveaxis(green_less, 1, 0)))
    collision = jnp.moveaxis(products, 0, 1) * (NT ** -0.5)
    return collision, green_less + collision
```

```python
import functools
import math

import jax
import jax.numpy as jnp
from jax import lax
from jax.experimental import pallas as pl
from jax.experimental.pallas import tpu as pltpu
from jax.sharding import PartitionSpec as P

MESH = pl.DeviceIdType.MESH
CHUNKS = 2
ROWS = 512
COLS = 256
CROWS = ROWS // CHUNKS
ZROWS = CROWS // 4
TROWS = ZROWS // 8
INNER = 32.0 ** -0.5
OUTER = 1.0 / (32.0 * math.sqrt(32.0) * 32.0)


def cmul(value, turns):
    turns = turns % 32
    re, im = value
    if turns == 0:
        return value
    if turns == 8:
        return -im, re
    if turns == 16:
        return -re, -im
    if turns == 24:
        return im, -re
    cos, sin = math.cos(2 * math.pi * turns / 32), math.sin(2 * math.pi * turns / 32)
    if turns % 8 == 4:
        root = math.sqrt(0.5)
        plus, minus = (re + im) * root, (re - im) * root
        return {4: (minus, plus), 12: (-plus, minus), 20: (-minus, -plus), 28: (plus, -minus)}[turns]
    return re * cos - im * sin, re * sin + im * cos


def cadd(a, b):
    return a[0] + b[0], a[1] + b[1]


def csub(a, b):
    return a[0] - b[0], a[1] - b[1]


def dft(values, sign):
    size = len(values)
    if size == 1:
        return values
    even, odd = dft(values[0::2], sign), dft(values[1::2], sign)
    step = 32 // size
    low, high = [], []
    for m in range(size // 2):
        turned = cmul(odd[m], sign * step * m)
        low.append(cadd(even[m], turned))
        high.append(csub(even[m], turned))
    return low + high


def split(value):
    high = value.astype(jnp.bfloat16)
    return high, (value - high.astype(jnp.float32)).astype(jnp.bfloat16)


def kernel(
    less, great, screen, collision, green_next,
    zbuf, tile, mid, mid2, sig, back, sigma, gloc, grem, ghigh, glow, acc,
    own_sem, zs, zr, xs, xr, ts, tr_, bs, br, cs, cr, ys, yr, fs, fr,
):
    ka, h, y = lax.axis_index("ka"), lax.axis_index("tr"), lax.axis_index("tc")
    x, z, c = ka // 8, (ka // 2) % 4, ka % 2
    xc = x * 2 + c

    def at(xx, zz, cc):
        return xx * 8 + zz * 2 + cc

    zpeers = [3 - z, (z + 2) % 4, z + 1 - 2 * (z % 2)]
    xpeers = [((x + 1) % 4, c), ((x + 3) % 4, 1 - c), ((x + 1) % 4, 1 - c), ((x + 3) % 4, c), ((x + 2) % 4, c), ((x + 2) % 4, 1 - c), (x, 1 - c)]
    up, down = (y + 1) % 4, (y + 3) % 4

    barrier = pltpu.get_barrier_semaphore()
    peers = [(at(x, zz, c), h, y) for zz in zpeers]
    peers += [(at(x, zz, c), 1 - h, y) for zz in range(4)]
    peers += [(at(xx, z, cc), h, y) for xx, cc in xpeers]
    peers += [(ka, h, up), (ka, h, down)]
    for peer in peers:
        pl.semaphore_signal(barrier, inc=1, device_id=peer, device_id_type=MESH)
    pl.semaphore_wait(barrier, len(peers))

    arrays = (less, great, screen)
    pending = []

    def remote(src, dst, send, recv, peer):
        copy = pltpu.make_async_remote_copy(
            src_ref=src, dst_ref=dst, send_sem=send, recv_sem=recv, device_id=peer, device_id_type=MESH
        )
        copy.start()
        pending.append(copy)

    def arrived(ref, sem, send):
        pltpu.make_async_remote_copy(
            src_ref=ref, dst_ref=ref, send_sem=send, recv_sem=sem, device_id=(ka, h, y), device_id_type=MESH
        ).wait_recv()

    def rows(start, size):
        return pl.ds(pl.multiple_of(start, 8), size)

    load = pltpu.make_async_copy(less.at[:, 0], gloc, own_sem.at[0])
    for n in range(CHUNKS):
        for a in range(3):
            for i, zz in enumerate(zpeers):
                remote(
                    arrays[a].at[:, 0, rows(n * CROWS + zz * ZROWS, ZROWS), :],
                    zbuf.at[n, a, z], zs.at[n, a, i], zr.at[n, a, i], (at(x, zz, c), h, y),
                )
    own = [
        [
            pltpu.make_async_copy(
                arrays[a].at[:, 0, rows(n * CROWS + z * ZROWS, ZROWS), :], zbuf.at[n, a, z], own_sem.at[1 + 3 * n + a]
            )
            for a in range(3)
        ]
        for n in range(CHUNKS)
    ]
    for n in range(CHUNKS):
        for a in range(3):
            own[n][a].start()
    load.start()

    def forward_x(n, a):
        own[n][a].wait()
        for i, zz in enumerate(zpeers):
            arrived(zbuf.at[n, a, zz], zr.at[n, a, i], zs.at[n, a, i])
        for i, (xx, cc) in enumerate(xpeers):
            remote(
                zbuf.at[n, a, :, :, rows((xx * 2 + cc) * TROWS, TROWS), :],
                tile.at[n, a, xc], xs.at[n, a, i], xr.at[n, a, i], (at(xx, z, cc), h, y),
            )
        tile[n, a, xc] = zbuf[n, a, :, :, rows(xc * TROWS, TROWS), :]

    mirror = [3, 2, 1, 0, 4, 5, 6]
    mirror = [3, 2, 1, 0, 4, 5, 6]

    def transform(n):
        for a in range(3):
            for i in range(7):
                sender_xx, sender_cc = xpeers[mirror_of[i]]
                arrived(tile.at[n, a, sender_xx * 2 + sender_cc], xr.at[n, a, i], xs.at[n, a, i])

        def column(q, carry):
            cols = pl.ds(pl.multiple_of(q * 128, 128), 128)

            for a in range(3):
                for k2 in range(8):
                    j, cc = k2 // 2, k2 % 2
                    values = [
                        (tile[n, a, 2 * xx + cc, j, 0, :, cols], tile[n, a, 2 * xx + cc, j, 1, :, cols])
                        for xx in range(4)
                    ]
                    for r1, value in enumerate(dft(values, 1)):
                        re, im = cmul(value, k2 * r1)
                        mid[a, r1, k2, 0], mid[a, r1, k2, 1] = re, im
            for r1 in range(4):
                sides = [dft([(mid[a, r1, k2, 0], mid[a, r1, k2, 1]) for k2 in range(8)], 1) for a in range(3)]
                out = []
                for (lr, li), (gr, gi), (wr, wi) in zip(*sides):
                    ir = OUTER * wr + (OUTER * INNER) * (lr * gi - li * gr)
                    ii = OUTER * wi + (OUTER * INNER) * (lr * gr + li * gi)
                    out.append((-(lr * ii + li * ir), lr * ir - li * ii))
                for k2, value in enumerate(dft(out, -1)):
                    re, im = cmul(value, -k2 * r1)
                    mid2[r1, k2, 0], mid2[r1, k2, 1] = re, im
            for k2 in range(8):
                j, cc = k2 // 2, k2 % 2
                for xx, (re, im) in enumerate(dft([(mid2[r1, k2, 0], mid2[r1, k2, 1]) for r1 in range(4)], -1)):
                    sig[n, 2 * xx + cc, j, 0, :, cols] = re
                    sig[n, 2 * xx + cc, j, 1, :, cols] = im
            return carry

        lax.fori_loop(0, COLS // 128, column, 0)
        for i, (xx, cc) in enumerate(xpeers):
            remote(
                sig.at[n, xx * 2 + cc], back.at[n, :, :, rows(xc * TROWS, TROWS), :],
                bs.at[n, i], br.at[n, i], (at(xx, z, cc), h, y),
            )
        back[n, :, :, rows(xc * TROWS, TROWS), :] = sig[n, xc]

    mirror_of = mirror

    def back_z(n):
        for i in range(7):
            sender_xx, sender_cc = xpeers[mirror_of[i]]
            arrived(back.at[n, :, :, rows((sender_xx * 2 + sender_cc) * TROWS, TROWS), :], br.at[n, i], bs.at[n, i])
        for i, zz in enumerate(zpeers):
            remote(
                back.at[n, zz], sigma.at[y, :, rows(n * CROWS + z * ZROWS, ZROWS), :],
                cs.at[n, i], cr.at[n, i], (at(x, zz, c), h, y),
            )
        sigma[y, :, rows(n * CROWS + z * ZROWS, ZROWS), :] = back[n, z]

    def share_less(n):
        for i, zz in enumerate([z] + zpeers):
            remote(
                zbuf.at[n, 0, zz], grem.at[:, rows(n * CROWS + z * ZROWS, ZROWS), :],
                ts.at[n, i], tr_.at[n, i], (at(x, zz, c), 1 - h, y),
            )

    def wait_less(n):
        for i, zz in enumerate([z] + zpeers):
            arrived(grem.at[:, rows(n * CROWS + zz * ZROWS, ZROWS), :], tr_.at[n, i], ts.at[n, i])

    def spread_y(n):
        for i, zz in enumerate(zpeers):
            arrived(sigma.at[y, :, rows(n * CROWS + zz * ZROWS, ZROWS), :], cr.at[n, i], cs.at[n, i])
        block = sigma.at[y, :, pl.ds(n * CROWS, CROWS), :]
        remote(block, block, ys.at[n, 0], yr.at[n, 0], (ka, h, up))
        remote(block, block, ys.at[n, 1], yr.at[n, 1], (ka, h, down))

    def relay_y(n):
        half = CROWS // 2
        arrived(sigma.at[down, :, pl.ds(n * CROWS, CROWS), :], yr.at[n, 0], ys.at[n, 0])
        block = sigma.at[down, :, pl.ds(n * CROWS, half), :]
        remote(block, block, fs.at[n, 0], fr.at[n, 0], (ka, h, up))
        arrived(sigma.at[up, :, pl.ds(n * CROWS, CROWS), :], yr.at[n, 1], ys.at[n, 1])
        block = sigma.at[up, :, pl.ds(n * CROWS + half, half), :]
        remote(block, block, fs.at[n, 1], fr.at[n, 1], (ka, h, down))

    def wait_y(n):
        half = CROWS // 2
        far = (y + 2) % 4
        arrived(sigma.at[far, :, pl.ds(n * CROWS, half), :], fr.at[n, 0], fs.at[n, 0])
        arrived(sigma.at[far, :, pl.ds(n * CROWS + half, half), :], fr.at[n, 1], fs.at[n, 1])

    def prepare(source, part):
        for s in range(2):
            re, im = source[0, s * 256:(s + 1) * 256, :], source[1, s * 256:(s + 1) * 256, :]
            for value, places in ((re, ((0, 0), (1, 256))), (im, ((0, 256),)), (-im, ((1, 0),))):
                high, low = split(value)
                for ri, col in places:
                    ghigh[part * 2 + s, ri, :, col:col + 256] = high
                    glow[part * 2 + s, ri, :, col:col + 256] = low

    def multiply(n, part, first):
        def block(s, carry):
            index = part * 2 + s
            total = None
            for ri in range(2):
                high, low = split(sigma[index, ri, pl.ds(n * CROWS, CROWS), :])
                for left, right in ((high, ghigh), (high, glow), (low, ghigh)):
                    product = jnp.dot(left, right[index, ri], preferred_element_type=jnp.float32)
                    total = product if total is None else total + product
            acc[n] += total
            return carry

        if first:
            acc[n] = jnp.zeros_like(acc[n])
        lax.fori_loop(0, 2, block, 0)

    def finish(n):
        span = pl.ds(n * CROWS, CROWS)
        for ri in range(2):
            value = acc[n, :, ri * 256:(ri + 1) * 256]
            collision[ri, 0, span, :] = value
            green_next[ri, 0, span, :] = gloc[ri, span, :] + value

    load.wait()
    prepare(gloc, h)
    forward_x(0, 0)
    forward_x(0, 1)
    forward_x(0, 2)
    transform(0)
    forward_x(1, 0)
    back_z(0)
    share_less(0)
    forward_x(1, 1)
    forward_x(1, 2)
    transform(1)
    back_z(1)
    share_less(1)
    spread_y(0)
    relay_y(0)
    spread_y(1)
    wait_y(0)
    multiply(0, h, True)
    relay_y(1)
    wait_less(0)
    wait_less(1)
    prepare(grem, 1 - h)
    multiply(0, 1 - h, False)
    finish(0)
    wait_y(1)
    multiply(1, h, True)
    multiply(1, 1 - h, False)
    finish(1)
    for copy in pending:
        copy.wait_send()


def body(green_less, green_great, screened):
    dma = pltpu.SemaphoreType.DMA
    block = jax.ShapeDtypeStruct(green_less.shape, jnp.float32)
    f32, bf16 = jnp.float32, jnp.bfloat16
    return pl.pallas_call(
        kernel,
        out_shape=(block, block),
        in_specs=[pl.BlockSpec(memory_space=pl.ANY)] * 3,
        out_specs=(pl.BlockSpec(memory_space=pltpu.VMEM),) * 2,
        scratch_shapes=[
            pltpu.VMEM((CHUNKS, 3, 4, 2, ZROWS, COLS), f32),
            pltpu.VMEM((CHUNKS, 3, 8, 4, 2, TROWS, COLS), f32),
            pltpu.VMEM((3, 4, 8, 2, TROWS, 128), f32),
            pltpu.VMEM((4, 8, 2, TROWS, 128), f32),
            pltpu.VMEM((CHUNKS, 8, 4, 2, TROWS, COLS), f32),
            pltpu.VMEM((CHUNKS, 4, 2, ZROWS, COLS), f32),
            pltpu.VMEM((4, 2, ROWS, COLS), f32),
            pltpu.VMEM((2, ROWS, COLS), f32),
            pltpu.VMEM((2, ROWS, COLS), f32),
            pltpu.VMEM((4, 2, 256, 512), bf16),
            pltpu.VMEM((4, 2, 256, 512), bf16),
            pltpu.VMEM((CHUNKS, CROWS, 512), f32),
            dma((1 + 3 * CHUNKS,)),
            dma((CHUNKS, 3, 3)), dma((CHUNKS, 3, 3)),
            dma((CHUNKS, 3, 7)), dma((CHUNKS, 3, 7)),
            dma((CHUNKS, 4)), dma((CHUNKS, 4)),
            dma((CHUNKS, 7)), dma((CHUNKS, 7)),
            dma((CHUNKS, 3)), dma((CHUNKS, 3)),
            dma((CHUNKS, 2)), dma((CHUNKS, 2)),
            dma((CHUNKS, 2)), dma((CHUNKS, 2)),
        ],
        compiler_params=pltpu.CompilerParams(collective_id=0, has_side_effects=True, vmem_limit_bytes=56 << 20),
        name="collide",
    )(green_less, green_great, screened)


def solution(mesh):
    spec = P(None, "ka", "tr", "tc")
    return jax.shard_map(body, mesh=mesh, in_specs=(spec,) * 3, out_specs=(spec,) * 2, check_vma=False)
```

```python
import functools
import math

import jax
import jax.numpy as jnp
from jax import lax
from jax.experimental import pallas as pl
from jax.experimental.pallas import tpu as pltpu
from jax.sharding import PartitionSpec as P

MESH = pl.DeviceIdType.MESH
ROWS = 512
COLS = 256
CHUNKS = 4
CROWS = 256
CCOLS = 128
ZROWS = CROWS // 4
TROWS = ZROWS // 8
INNER = 32.0 ** -0.5
OUTER = 1.0 / (32.0 * math.sqrt(32.0))
NORM = 1.0 / 32.0


def cmul(value, turns):
    turns = turns % 32
    re, im = value
    if turns == 0:
        return value
    if turns == 8:
        return -im, re
    if turns == 16:
        return -re, -im
    if turns == 24:
        return im, -re
    cos, sin = math.cos(2 * math.pi * turns / 32), math.sin(2 * math.pi * turns / 32)
    if turns % 8 == 4:
        root = math.sqrt(0.5)
        plus, minus = (re + im) * root, (re - im) * root
        return {4: (minus, plus), 12: (-plus, minus), 20: (-minus, -plus), 28: (plus, -minus)}[turns]
    return re * cos - im * sin, re * sin + im * cos


def cadd(a, b):
    return a[0] + b[0], a[1] + b[1]


def csub(a, b):
    return a[0] - b[0], a[1] - b[1]


def dft(values, sign):
    size = len(values)
    if size == 1:
        return values
    even, odd = dft(values[0::2], sign), dft(values[1::2], sign)
    step = 32 // size
    low, high = [], []
    for m in range(size // 2):
        turned = cmul(odd[m], sign * step * m)
        low.append(cadd(even[m], turned))
        high.append(csub(even[m], turned))
    return low + high


def split(value):
    high = value.astype(jnp.bfloat16)
    return high, (value - high.astype(jnp.float32)).astype(jnp.bfloat16)


def kernel(
    less, great, screen, product,
    zbuf, tile, mid, mid2, sig, back, sigma, gloc, grem, ghigh, glow, acc,
    own_sem, out_sem, zs, zr, xs, xr, ts, tr, bs, br, cs, cr, ys, yr, fs, fr,
):
    ka, h, y = lax.axis_index("ka"), lax.axis_index("tr"), lax.axis_index("tc")
    x, z, c = ka // 8, (ka // 2) % 4, ka % 2
    xc = x * 2 + c
    arrays = (less, great, screen)
    pending = []

    def at(xx, zz, cc):
        return xx * 8 + zz * 2 + cc

    zpeers = [3 - z, (z + 2) % 4, z + 1 - 2 * (z % 2)]
    xpeers = [
        ((x + 1) % 4, c), ((x + 3) % 4, 1 - c), ((x + 1) % 4, 1 - c), ((x + 3) % 4, c),
        ((x + 2) % 4, c), ((x + 2) % 4, 1 - c), (x, 1 - c),
    ]
    opposite = [3, 2, 1, 0, 4, 5, 6]
    up, down = (y + 1) % 4, (y + 3) % 4

    def remote(src, dst, send, recv, peer):
        copy = pltpu.make_async_remote_copy(
            src_ref=src, dst_ref=dst, send_sem=send, recv_sem=recv, device_id=peer, device_id_type=MESH
        )
        copy.start()
        pending.append(copy)

    def arrived(ref, sem, send):
        pltpu.make_async_remote_copy(
            src_ref=ref, dst_ref=ref, send_sem=send, recv_sem=sem, device_id=(ka, h, y), device_id_type=MESH
        ).wait_recv()

    def rows(start, size):
        return pl.ds(pl.multiple_of(start, 8), size)

    def zrows(m, zz):
        return rows((m // 2) * CROWS + zz * ZROWS, ZROWS)

    def cols(m):
        return pl.ds((m % 2) * CCOLS, CCOLS)

    def xrows(index):
        return rows(index * TROWS, TROWS)

    own = [
        [
            pltpu.make_async_copy(arrays[a].at[:, 0, zrows(m, z), cols(m)], zbuf.at[m, a, z], own_sem.at[1 + 3 * m + a])
            for a in range(3)
        ]
        for m in range(CHUNKS)
    ]
    load = pltpu.make_async_copy(less.at[:, 0], gloc, own_sem.at[0])

    def send_z(m, a):
        for i, zz in enumerate(zpeers):
            remote(
                arrays[a].at[:, 0, zrows(m, zz), cols(m)], zbuf.at[m, a, z],
                zs.at[m, a, i], zr.at[m, a, i], (at(x, zz, c), h, y),
            )

    def send_x(m, a):
        own[m][a].wait()
        for i, zz in enumerate(zpeers):
            arrived(zbuf.at[m, a, zz], zr.at[m, a, i], zs.at[m, a, i])
        for i, (xx, cc) in enumerate(xpeers):
            remote(
                zbuf.at[m, a, :, :, xrows(xx * 2 + cc), :], tile.at[m, a, xc],
                xs.at[m, a, i], xr.at[m, a, i], (at(xx, z, cc), h, y),
            )
        tile[m, a, xc] = zbuf[m, a, :, :, xrows(xc), :]

    def arrive_z(m, a):
        own[m][a].wait()
        for i, zz in enumerate(zpeers):
            arrived(zbuf.at[m, a, zz], zr.at[m, a, i], zs.at[m, a, i])

    def arrive_x(m, a):
        for i in range(7):
            xx, cc = xpeers[opposite[i]]
            arrived(tile.at[m, a, xx * 2 + cc], xr.at[m, a, i], xs.at[m, a, i])

    def arrive_c(m):
        for i, zz in enumerate(zpeers):
            arrived(sigma.at[y, m % 2, :, zrows(m, zz), :], cr.at[m, i], cs.at[m, i])

    def share_less(m):
        for i, zz in enumerate([z] + zpeers):
            remote(
                zbuf.at[m, 0, zz], grem.at[:, zrows(m, z), cols(m)],
                ts.at[m, i], tr.at[m, i], (at(x, zz, c), 1 - h, y),
            )

    def wait_less(m):
        for i, zz in enumerate([z] + zpeers):
            arrived(grem.at[:, zrows(m, zz), cols(m)], tr.at[m, i], ts.at[m, i])

    def transform(m):
        for a in range(3):
            for i in range(7):
                xx, cc = xpeers[opposite[i]]
                arrived(tile.at[m, a, xx * 2 + cc], xr.at[m, a, i], xs.at[m, a, i])
        for a in range(3):
            for k2 in range(8):
                j, cc = k2 // 2, k2 % 2
                values = [(tile[m, a, 2 * xx + cc, j, 0], tile[m, a, 2 * xx + cc, j, 1]) for xx in range(4)]
                for r1, value in enumerate(dft(values, 1)):
                    mid[a, r1, k2, 0], mid[a, r1, k2, 1] = cmul(value, k2 * r1)
        for r1 in range(4):
            sides = [dft([(mid[a, r1, k2, 0], mid[a, r1, k2, 1]) for k2 in range(8)], 1) for a in range(3)]
            out = []
            for (lr, li), (gr, gi), (wr, wi) in zip(*sides):
                ir = OUTER * wr + (OUTER * INNER) * (lr * gi - li * gr)
                ii = OUTER * wi + (OUTER * INNER) * (lr * gr + li * gi)
                out.append((-(lr * ii + li * ir), lr * ir - li * ii))
            for k2, value in enumerate(dft(out, -1)):
                mid2[r1, k2, 0], mid2[r1, k2, 1] = cmul(value, -k2 * r1)
        for k2 in range(8):
            j, cc = k2 // 2, k2 % 2
            for xx, value in enumerate(dft([(mid2[r1, k2, 0], mid2[r1, k2, 1]) for r1 in range(4)], -1)):
                sig[m, 2 * xx + cc, j, 0], sig[m, 2 * xx + cc, j, 1] = value
        for i, (xx, cc) in enumerate(xpeers):
            remote(
                sig.at[m, xx * 2 + cc], back.at[m, :, :, xrows(xc), :], bs.at[m, i], br.at[m, i], (at(xx, z, cc), h, y)
            )
        back[m, :, :, xrows(xc), :] = sig[m, xc]

    def back_z(m):
        for i in range(7):
            xx, cc = xpeers[opposite[i]]
            arrived(back.at[m, :, :, xrows(xx * 2 + cc), :], br.at[m, i], bs.at[m, i])
        for i, zz in enumerate(zpeers):
            remote(back.at[m, zz], sigma.at[y, m % 2, :, zrows(m, z), :], cs.at[m, i], cr.at[m, i], (at(x, zz, c), h, y))
        sigma[y, m % 2, :, zrows(m, z), :] = back[m, z]

    pieces = [z] + zpeers

    def piece(yy, m, i):
        return sigma.at[yy, m % 2, :, zrows(m, pieces[i]), :]

    def spread_y(m, i):
        if i > 0:
            arrived(piece(y, m, i), cr.at[m, i - 1], cs.at[m, i - 1])
        remote(piece(y, m, i), piece(y, m, i), ys.at[m, i, 0], yr.at[m, i, 0], (ka, h, up))
        remote(piece(y, m, i), piece(y, m, i), ys.at[m, i, 1], yr.at[m, i, 1], (ka, h, down))

    def relay_y(m, i):
        arrived(piece(down, m, i), yr.at[m, i, 0], ys.at[m, i, 0])
        if i % 2 == 0:
            remote(piece(down, m, i), piece(down, m, i), fs.at[m, i], fr.at[m, i], (ka, h, up))
        arrived(piece(up, m, i), yr.at[m, i, 1], ys.at[m, i, 1])
        if i % 2 == 1:
            remote(piece(up, m, i), piece(up, m, i), fs.at[m, i], fr.at[m, i], (ka, h, down))

    def wait_y(m):
        for i in range(4):
            arrived(piece((y + 2) % 4, m, i), fr.at[m, i], fs.at[m, i])

    def prepare(source, part, blocks):
        for s in blocks:
            re, im = source[0, s * 128:(s + 1) * 128, :], source[1, s * 128:(s + 1) * 128, :]
            for value, places in ((re, ((0, 0), (128, 256))), (im, ((0, 256),)), (-im, ((128, 0),))):
                high, low = split(value)
                for row, col in places:
                    ghigh[part * 4 + s, row:row + 128, col:col + 256] = high
                    glow[part * 4 + s, row:row + 128, col:col + 256] = low

    def multiply(m, part, first, last):
        def block(s, carry):
            multiply_one(m, part * 2 + s)
            return carry

        lax.fori_loop(first, last, block, 0)

    def multiply_one(m, yy):
        span = pl.ds((m // 2) * CROWS, CROWS)
        left = jnp.concatenate([sigma[yy, m % 2, 0, span, :], sigma[yy, m % 2, 1, span, :]], axis=1)
        high, low = split(left)
        index = yy * 2 + m % 2
        total = jnp.dot(high, ghigh[index], preferred_element_type=jnp.float32)
        total += jnp.dot(high, glow[index], preferred_element_type=jnp.float32)
        total += jnp.dot(low, ghigh[index], preferred_element_type=jnp.float32)
        acc[m // 2] += total

    results = []

    def finish(n):
        span = pl.ds(n * CROWS, CROWS)
        for ri in range(2):
            copy = pltpu.make_async_copy(
                acc.at[n, :, pl.ds(ri * 256, 256)], product.at[ri, 0, span, :], out_sem.at[n, ri]
            )
            copy.start()
            results.append(copy)

    for a in range(3):
        for m in range(CHUNKS):
            own[m][a].start()
    load.start()
    barrier = pltpu.get_barrier_semaphore()
    peers = [(at(x, zz, c), h, y) for zz in zpeers]
    peers += [(at(x, zz, c), 1 - h, y) for zz in range(4)]
    peers += [(at(xx, z, cc), h, y) for xx, cc in xpeers]
    peers += [(ka, h, up), (ka, h, down)]
    for peer in peers:
        pl.semaphore_signal(barrier, inc=1, device_id=peer, device_id_type=MESH)
    pl.semaphore_wait(barrier, len(peers))

    send_z(0, 0)
    send_z(0, 1)
    send_z(0, 2)
    send_z(1, 0)
    acc[...] = jnp.zeros_like(acc)
    load.wait()
    prepare(gloc, h, range(4))
    send_x(0, 0)
    send_z(1, 1)
    share_less(0)
    send_x(0, 1)
    send_z(1, 2)
    send_z(2, 0)
    send_x(0, 2)
    send_z(2, 1)
    send_x(1, 0)
    transform(0)
    send_x(1, 1)
    back_z(0)
    send_z(2, 2)
    share_less(1)
    send_x(1, 2)
    send_z(3, 0)
    send_x(2, 0)
    send_z(3, 1)
    transform(1)
    send_x(2, 1)
    back_z(1)
    send_z(3, 2)
    spread_y(0, 0)
    spread_y(0, 1)
    spread_y(0, 2)
    spread_y(0, 3)
    send_x(2, 2)
    relay_y(0, 0)
    relay_y(0, 1)
    relay_y(0, 2)
    relay_y(0, 3)
    send_x(3, 0)
    transform(2)
    spread_y(1, 0)
    spread_y(1, 1)
    spread_y(1, 2)
    spread_y(1, 3)
    send_x(3, 1)
    back_z(2)
    share_less(2)
    wait_y(0)
    multiply(0, h, 0, 2)
    send_x(3, 2)
    transform(3)
    relay_y(1, 0)
    relay_y(1, 1)
    relay_y(1, 2)
    relay_y(1, 3)
    spread_y(2, 0)
    spread_y(2, 1)
    spread_y(2, 2)
    spread_y(2, 3)
    back_z(3)
    share_less(3)
    wait_less(0)
    wait_less(1)
    prepare(grem, 1 - h, range(0, 2))
    wait_y(1)
    multiply(1, h, 0, 2)
    multiply(0, 1 - h, 0, 1)
    multiply(1, 1 - h, 0, 1)
    relay_y(2, 0)
    relay_y(2, 1)
    relay_y(2, 2)
    relay_y(2, 3)
    spread_y(3, 0)
    spread_y(3, 1)
    spread_y(3, 2)
    spread_y(3, 3)
    relay_y(3, 0)
    wait_y(2)
    multiply(2, h, 0, 2)
    multiply(2, 1 - h, 0, 1)
    relay_y(3, 1)
    relay_y(3, 2)
    relay_y(3, 3)
    wait_less(2)
    wait_less(3)
    prepare(grem, 1 - h, range(2, 4))
    multiply(0, 1 - h, 1, 2)
    multiply(1, 1 - h, 1, 2)
    finish(0)
    multiply(2, 1 - h, 1, 2)
    multiply_one(3, y)
    multiply_one(3, up)
    multiply_one(3, down)
    wait_y(3)
    multiply_one(3, (y + 2) % 4)
    finish(1)
    for copy in results:
        copy.wait()
    for copy in pending:
        copy.wait_send()


def body(green_less, green_great, screened):
    dma = pltpu.SemaphoreType.DMA
    block = jax.ShapeDtypeStruct(green_less.shape, jnp.float32)
    f32, bf16 = jnp.float32, jnp.bfloat16
    product = pl.pallas_call(
        kernel,
        out_shape=block,
        in_specs=[pl.BlockSpec(memory_space=pl.ANY)] * 3,
        out_specs=pl.BlockSpec(memory_space=pl.ANY),
        scratch_shapes=[
            pltpu.VMEM((CHUNKS, 3, 4, 2, ZROWS, CCOLS), f32),
            pltpu.VMEM((CHUNKS, 3, 8, 4, 2, TROWS, CCOLS), f32),
            pltpu.VMEM((3, 4, 8, 2, TROWS, CCOLS), f32),
            pltpu.VMEM((4, 8, 2, TROWS, CCOLS), f32),
            pltpu.VMEM((CHUNKS, 8, 4, 2, TROWS, CCOLS), f32),
            pltpu.VMEM((CHUNKS, 4, 2, ZROWS, CCOLS), f32),
            pltpu.VMEM((4, 2, 2, ROWS, CCOLS), f32),
            pltpu.VMEM((2, ROWS, COLS), f32),
            pltpu.VMEM((2, ROWS, COLS), f32),
            pltpu.VMEM((8, 256, 512), bf16),
            pltpu.VMEM((8, 256, 512), bf16),
            pltpu.VMEM((2, CROWS, 512), f32),
            dma((1 + 3 * CHUNKS,)), dma((2, 2)),
            dma((CHUNKS, 3, 3)), dma((CHUNKS, 3, 3)),
            dma((CHUNKS, 3, 7)), dma((CHUNKS, 3, 7)),
            dma((CHUNKS, 4)), dma((CHUNKS, 4)),
            dma((CHUNKS, 7)), dma((CHUNKS, 7)),
            dma((CHUNKS, 3)), dma((CHUNKS, 3)),
            dma((CHUNKS, 4, 2)), dma((CHUNKS, 4, 2)),
            dma((CHUNKS, 4)), dma((CHUNKS, 4)),
        ],
        compiler_params=pltpu.CompilerParams(collective_id=0, has_side_effects=True, vmem_limit_bytes=56 << 20),
        name="collide",
    )(green_less, green_great, screened)
    collision = product * NORM
    return collision, green_less + collision


def solution(mesh):
    spec = P(None, "ka", "tr", "tc")
    return jax.shard_map(body, mesh=mesh, in_specs=(spec,) * 3, out_specs=(spec,) * 2, check_vma=False)
```

```python
import functools
import math

import jax
import jax.numpy as jnp
from jax import lax
from jax.experimental import pallas as pl
from jax.experimental.pallas import tpu as pltpu
from jax.sharding import PartitionSpec as P

MESH = pl.DeviceIdType.MESH
ROWS = 512
COLS = 256
CHUNKS = 4
CROWS = 256
CCOLS = 128
ZROWS = CROWS // 4
TROWS = ZROWS // 8
INNER = 32.0 ** -0.5
OUTER = 1.0 / (32.0 * math.sqrt(32.0))
NORM = 1.0 / 32.0


def cmul(value, turns):
    turns = turns % 32
    re, im = value
    if turns == 0:
        return value
    if turns == 8:
        return -im, re
    if turns == 16:
        return -re, -im
    if turns == 24:
        return im, -re
    cos, sin = math.cos(2 * math.pi * turns / 32), math.sin(2 * math.pi * turns / 32)
    if turns % 8 == 4:
        root = math.sqrt(0.5)
        plus, minus = (re + im) * root, (re - im) * root
        return {4: (minus, plus), 12: (-plus, minus), 20: (-minus, -plus), 28: (plus, -minus)}[turns]
    return re * cos - im * sin, re * sin + im * cos


def cadd(a, b):
    return a[0] + b[0], a[1] + b[1]


def csub(a, b):
    return a[0] - b[0], a[1] - b[1]


def dft(values, sign):
    size = len(values)
    if size == 1:
        return values
    even, odd = dft(values[0::2], sign), dft(values[1::2], sign)
    step = 32 // size
    low, high = [], []
    for m in range(size // 2):
        turned = cmul(odd[m], sign * step * m)
        low.append(cadd(even[m], turned))
        high.append(csub(even[m], turned))
    return low + high


def split(value):
    high = value.astype(jnp.bfloat16)
    return high, (value - high.astype(jnp.float32)).astype(jnp.bfloat16)


def kernel(
    less, great, screen, product,
    zbuf, tile, mid, mid2, sig, back, sigma, gloc, grem, ghigh, glow, acc,
    own_sem, out_sem, zs, zr, xs, xr, ts, tr, bs, br, cs, cr, ys, yr, fs, fr,
):
    ka, h, y = lax.axis_index("ka"), lax.axis_index("tr"), lax.axis_index("tc")
    x, z, c = ka // 8, (ka // 2) % 4, ka % 2
    xc = x * 2 + c
    arrays = (less, great, screen)
    pending = []

    def at(xx, zz, cc):
        return xx * 8 + zz * 2 + cc

    zpeers = [3 - z, (z + 2) % 4, z + 1 - 2 * (z % 2)]
    xpeers = [
        ((x + 1) % 4, c), ((x + 3) % 4, 1 - c), ((x + 1) % 4, 1 - c), ((x + 3) % 4, c),
        ((x + 2) % 4, c), ((x + 2) % 4, 1 - c), (x, 1 - c),
    ]
    opposite = [3, 2, 1, 0, 4, 5, 6]
    up, down = (y + 1) % 4, (y + 3) % 4

    def remote(src, dst, send, recv, peer):
        copy = pltpu.make_async_remote_copy(
            src_ref=src, dst_ref=dst, send_sem=send, recv_sem=recv, device_id=peer, device_id_type=MESH
        )
        copy.start()
        pending.append(copy)

    def arrived(ref, sem, send):
        pltpu.make_async_remote_copy(
            src_ref=ref, dst_ref=ref, send_sem=send, recv_sem=sem, device_id=(ka, h, y), device_id_type=MESH
        ).wait_recv()

    def rows(start, size):
        return pl.ds(pl.multiple_of(start, 8), size)

    def zrows(m, zz):
        return rows((m // 2) * CROWS + zz * ZROWS, ZROWS)

    def cols(m):
        return pl.ds((m % 2) * CCOLS, CCOLS)

    def xrows(index):
        return rows(index * TROWS, TROWS)

    own = [
        [
            pltpu.make_async_copy(arrays[a].at[:, 0, zrows(m, z), cols(m)], zbuf.at[m, a, z], own_sem.at[1 + 3 * m + a])
            for a in range(3)
        ]
        for m in range(CHUNKS)
    ]
    load = pltpu.make_async_copy(less.at[:, 0], gloc, own_sem.at[0])

    def send_z(m, a):
        for i, zz in enumerate(zpeers):
            remote(
                arrays[a].at[:, 0, zrows(m, zz), cols(m)], zbuf.at[m, a, z],
                zs.at[m, a, i], zr.at[m, a, i], (at(x, zz, c), h, y),
            )

    def send_x(m, a):
        own[m][a].wait()
        for i, zz in enumerate(zpeers):
            arrived(zbuf.at[m, a, zz], zr.at[m, a, i], zs.at[m, a, i])
        for i, (xx, cc) in enumerate(xpeers):
            remote(
                zbuf.at[m, a, :, :, xrows(xx * 2 + cc), :], tile.at[m, a, xc],
                xs.at[m, a, i], xr.at[m, a, i], (at(xx, z, cc), h, y),
            )
        tile[m, a, xc] = zbuf[m, a, :, :, xrows(xc), :]

    def share_less(m, places):
        for i, zz in enumerate([z] + zpeers):
            if i not in places:
                continue
            remote(
                zbuf.at[m, 0, zz], grem.at[:, zrows(m, z), cols(m)],
                ts.at[m, i], tr.at[m, i], (at(x, zz, c), 1 - h, y),
            )

    def wait_less(m):
        for i, zz in enumerate([z] + zpeers):
            arrived(grem.at[:, zrows(m, zz), cols(m)], tr.at[m, i], ts.at[m, i])

    def transform(m):
        for a in range(3):
            for i in range(7):
                xx, cc = xpeers[opposite[i]]
                arrived(tile.at[m, a, xx * 2 + cc], xr.at[m, a, i], xs.at[m, a, i])
        for a in range(3):
            for k2 in range(8):
                j, cc = k2 // 2, k2 % 2
                values = [(tile[m, a, 2 * xx + cc, j, 0], tile[m, a, 2 * xx + cc, j, 1]) for xx in range(4)]
                for r1, value in enumerate(dft(values, 1)):
                    mid[a, r1, k2, 0], mid[a, r1, k2, 1] = cmul(value, k2 * r1)
        for r1 in range(4):
            sides = [dft([(mid[a, r1, k2, 0], mid[a, r1, k2, 1]) for k2 in range(8)], 1) for a in range(3)]
            out = []
            for (lr, li), (gr, gi), (wr, wi) in zip(*sides):
                ir = OUTER * wr + (OUTER * INNER) * (lr * gi - li * gr)
                ii = OUTER * wi + (OUTER * INNER) * (lr * gr + li * gi)
                out.append((-(lr * ii + li * ir), lr * ir - li * ii))
            for k2, value in enumerate(dft(out, -1)):
                mid2[r1, k2, 0], mid2[r1, k2, 1] = cmul(value, -k2 * r1)
        for k2 in range(8):
            j, cc = k2 // 2, k2 % 2
            for xx, value in enumerate(dft([(mid2[r1, k2, 0], mid2[r1, k2, 1]) for r1 in range(4)], -1)):
                sig[m, 2 * xx + cc, j, 0], sig[m, 2 * xx + cc, j, 1] = value
        for i, (xx, cc) in enumerate(xpeers):
            remote(
                sig.at[m, xx * 2 + cc], back.at[m, :, :, xrows(xc), :], bs.at[m, i], br.at[m, i], (at(xx, z, cc), h, y)
            )
        back[m, :, :, xrows(xc), :] = sig[m, xc]

    def back_z(m):
        for i in range(7):
            xx, cc = xpeers[opposite[i]]
            arrived(back.at[m, :, :, xrows(xx * 2 + cc), :], br.at[m, i], bs.at[m, i])
        for i, zz in enumerate(zpeers):
            remote(back.at[m, zz], sigma.at[y, m % 2, :, zrows(m, z), :], cs.at[m, i], cr.at[m, i], (at(x, zz, c), h, y))
        sigma[y, m % 2, :, zrows(m, z), :] = back[m, z]

    pieces = [z] + zpeers

    def piece(yy, m, i):
        return sigma.at[yy, m % 2, :, zrows(m, pieces[i]), :]

    def spread_y(m, i):
        if i > 0:
            arrived(piece(y, m, i), cr.at[m, i - 1], cs.at[m, i - 1])
        remote(piece(y, m, i), piece(y, m, i), ys.at[m, i, 0], yr.at[m, i, 0], (ka, h, up))
        remote(piece(y, m, i), piece(y, m, i), ys.at[m, i, 1], yr.at[m, i, 1], (ka, h, down))

    def relay_y(m, i):
        arrived(piece(down, m, i), yr.at[m, i, 0], ys.at[m, i, 0])
        if i % 2 == 0:
            remote(piece(down, m, i), piece(down, m, i), fs.at[m, i], fr.at[m, i], (ka, h, up))
        arrived(piece(up, m, i), yr.at[m, i, 1], ys.at[m, i, 1])
        if i % 2 == 1:
            remote(piece(up, m, i), piece(up, m, i), fs.at[m, i], fr.at[m, i], (ka, h, down))

    def wait_y(m):
        for i in range(4):
            arrived(piece((y + 2) % 4, m, i), fr.at[m, i], fs.at[m, i])

    def prepare(source, part, blocks):
        for s in blocks:
            re, im = source[0, s * 128:(s + 1) * 128, :], source[1, s * 128:(s + 1) * 128, :]
            for value, places in ((re, ((0, 0), (128, 256))), (im, ((0, 256),)), (-im, ((128, 0),))):
                high, low = split(value)
                for row, col in places:
                    ghigh[part * 4 + s, row:row + 128, col:col + 256] = high
                    glow[part * 4 + s, row:row + 128, col:col + 256] = low

    def multiply(m, part, first, last):
        def block(s, carry):
            multiply_one(m, part * 2 + s)
            return carry

        lax.fori_loop(first, last, block, 0)

    def multiply_one(m, yy):
        span = pl.ds((m // 2) * CROWS, CROWS)
        left = jnp.concatenate([sigma[yy, m % 2, 0, span, :], sigma[yy, m % 2, 1, span, :]], axis=1)
        high, low = split(left)
        index = yy * 2 + m % 2
        total = jnp.dot(high, ghigh[index], preferred_element_type=jnp.float32)
        total += jnp.dot(high, glow[index], preferred_element_type=jnp.float32)
        total += jnp.dot(low, ghigh[index], preferred_element_type=jnp.float32)
        acc[m // 2] += total

    results = []

    def finish(n):
        span = pl.ds(n * CROWS, CROWS)
        for ri in range(2):
            copy = pltpu.make_async_copy(
                acc.at[n, :, pl.ds(ri * 256, 256)], product.at[ri, 0, span, :], out_sem.at[n, ri]
            )
            copy.start()
            results.append(copy)

    for a in range(3):
        for m in range(CHUNKS):
            own[m][a].start()
    load.start()
    barrier = pltpu.get_barrier_semaphore()
    peers = [(at(x, zz, c), h, y) for zz in zpeers]
    peers += [(at(x, zz, c), 1 - h, y) for zz in range(4)]
    peers += [(at(xx, z, cc), h, y) for xx, cc in xpeers]
    peers += [(ka, h, up), (ka, h, down)]
    for peer in peers:
        pl.semaphore_signal(barrier, inc=1, device_id=peer, device_id_type=MESH)
    pl.semaphore_wait(barrier, len(peers))

    send_z(0, 0)
    send_z(0, 1)
    send_z(0, 2)
    send_z(1, 0)
    acc[...] = jnp.zeros_like(acc)
    load.wait()
    prepare(gloc, h, range(4))
    send_x(0, 0)
    send_z(1, 1)
    share_less(0, (1, 2))
    send_x(0, 1)
    send_z(1, 2)
    send_x(0, 2)
    send_z(2, 0)
    send_x(1, 0)
    share_less(1, (1, 2))
    send_z(2, 1)
    transform(0)
    send_x(1, 1)
    send_z(2, 2)
    back_z(0)
    send_x(1, 2)
    send_z(3, 0)
    send_x(2, 0)
    share_less(2, (1, 2))
    send_z(3, 1)
    transform(1)
    send_x(2, 1)
    send_z(3, 2)
    back_z(1)
    send_x(2, 2)
    spread_y(0, 0)
    spread_y(0, 3)
    spread_y(0, 1)
    spread_y(0, 2)
    send_x(3, 0)
    share_less(3, (1, 2))
    share_less(0, (0, 3))
    transform(2)
    send_x(3, 1)
    relay_y(0, 0)
    relay_y(0, 3)
    relay_y(0, 1)
    relay_y(0, 2)
    back_z(2)
    send_x(3, 2)
    share_less(1, (0, 3))
    transform(3)
    spread_y(1, 0)
    spread_y(1, 3)
    spread_y(1, 1)
    spread_y(1, 2)
    wait_y(0)
    multiply(0, h, 0, 2)
    back_z(3)
    spread_y(2, 0)
    relay_y(1, 0)
    relay_y(1, 3)
    spread_y(2, 3)
    relay_y(1, 1)
    relay_y(1, 2)
    spread_y(2, 1)
    spread_y(2, 2)
    spread_y(3, 0)
    relay_y(2, 0)
    relay_y(2, 3)
    spread_y(3, 3)
    relay_y(2, 1)
    spread_y(3, 1)
    share_less(2, (0, 3))
    share_less(3, (0, 3))
    relay_y(2, 2)
    spread_y(3, 2)
    wait_y(1)
    multiply(1, h, 0, 2)
    wait_less(0)
    wait_less(1)
    prepare(grem, 1 - h, range(0, 2))
    multiply(0, 1 - h, 0, 1)
    multiply(1, 1 - h, 0, 1)
    relay_y(3, 0)
    relay_y(3, 3)
    relay_y(3, 1)
    relay_y(3, 2)
    wait_y(2)
    multiply(2, h, 0, 2)
    multiply(2, 1 - h, 0, 1)
    wait_less(2)
    wait_less(3)
    prepare(grem, 1 - h, range(2, 4))
    multiply(0, 1 - h, 1, 2)
    multiply(1, 1 - h, 1, 2)
    finish(0)
    multiply(2, 1 - h, 1, 2)
    multiply_one(3, y)
    multiply_one(3, up)
    multiply_one(3, down)
    wait_y(3)
    multiply_one(3, (y + 2) % 4)
    finish(1)
    for copy in results:
        copy.wait()
    for copy in pending:
        copy.wait_send()


def body(green_less, green_great, screened):
    dma = pltpu.SemaphoreType.DMA
    block = jax.ShapeDtypeStruct(green_less.shape, jnp.float32)
    f32, bf16 = jnp.float32, jnp.bfloat16
    product = pl.pallas_call(
        kernel,
        out_shape=block,
        in_specs=[pl.BlockSpec(memory_space=pl.ANY)] * 3,
        out_specs=pl.BlockSpec(memory_space=pl.ANY),
        scratch_shapes=[
            pltpu.VMEM((CHUNKS, 3, 4, 2, ZROWS, CCOLS), f32),
            pltpu.VMEM((CHUNKS, 3, 8, 4, 2, TROWS, CCOLS), f32),
            pltpu.VMEM((3, 4, 8, 2, TROWS, CCOLS), f32),
            pltpu.VMEM((4, 8, 2, TROWS, CCOLS), f32),
            pltpu.VMEM((CHUNKS, 8, 4, 2, TROWS, CCOLS), f32),
            pltpu.VMEM((CHUNKS, 4, 2, ZROWS, CCOLS), f32),
            pltpu.VMEM((4, 2, 2, ROWS, CCOLS), f32),
            pltpu.VMEM((2, ROWS, COLS), f32),
            pltpu.VMEM((2, ROWS, COLS), f32),
            pltpu.VMEM((8, 256, 512), bf16),
            pltpu.VMEM((8, 256, 512), bf16),
            pltpu.VMEM((2, CROWS, 512), f32),
            dma((1 + 3 * CHUNKS,)), dma((2, 2)),
            dma((CHUNKS, 3, 3)), dma((CHUNKS, 3, 3)),
            dma((CHUNKS, 3, 7)), dma((CHUNKS, 3, 7)),
            dma((CHUNKS, 4)), dma((CHUNKS, 4)),
            dma((CHUNKS, 7)), dma((CHUNKS, 7)),
            dma((CHUNKS, 3)), dma((CHUNKS, 3)),
            dma((CHUNKS, 4, 2)), dma((CHUNKS, 4, 2)),
            dma((CHUNKS, 4)), dma((CHUNKS, 4)),
        ],
        compiler_params=pltpu.CompilerParams(collective_id=0, has_side_effects=True, vmem_limit_bytes=52 << 20),
        name="collide",
    )(green_less, green_great, screened)
    collision = product * NORM
    return collision, green_less + collision


def solution(mesh):
    spec = P(None, "ka", "tr", "tc")
    return jax.shard_map(body, mesh=mesh, in_specs=(spec,) * 3, out_specs=(spec,) * 2, check_vma=False)
```

```python
import functools
import math

import jax
import jax.numpy as jnp
from jax import lax
from jax.experimental import pallas as pl
from jax.experimental.pallas import tpu as pltpu
from jax.sharding import PartitionSpec as P

MESH = pl.DeviceIdType.MESH
ROWS = 512
COLS = 256
CHUNKS = 4
CROWS = 256
CCOLS = 128
ZROWS = CROWS // 4
TROWS = ZROWS // 8
INNER = 32.0 ** -0.5
OUTER = 1.0 / (32.0 * math.sqrt(32.0))
NORM = 1.0 / 32.0


def cmul(value, turns):
    turns = turns % 32
    re, im = value
    if turns == 0:
        return value
    if turns == 8:
        return -im, re
    if turns == 16:
        return -re, -im
    if turns == 24:
        return im, -re
    cos, sin = math.cos(2 * math.pi * turns / 32), math.sin(2 * math.pi * turns / 32)
    if turns % 8 == 4:
        root = math.sqrt(0.5)
        plus, minus = (re + im) * root, (re - im) * root
        return {4: (minus, plus), 12: (-plus, minus), 20: (-minus, -plus), 28: (plus, -minus)}[turns]
    return re * cos - im * sin, re * sin + im * cos


def cadd(a, b):
    return a[0] + b[0], a[1] + b[1]


def csub(a, b):
    return a[0] - b[0], a[1] - b[1]


def dft(values, sign):
    size = len(values)
    if size == 1:
        return values
    even, odd = dft(values[0::2], sign), dft(values[1::2], sign)
    step = 32 // size
    low, high = [], []
    for m in range(size // 2):
        turned = cmul(odd[m], sign * step * m)
        low.append(cadd(even[m], turned))
        high.append(csub(even[m], turned))
    return low + high


def split(value):
    high = value.astype(jnp.bfloat16)
    return high, (value - high.astype(jnp.float32)).astype(jnp.bfloat16)


def kernel(
    less, great, screen, product,
    zbuf, tile, mid, mid2, sig, back, sigma, gloc, grem, ghigh, glow,
    own_sem, zs, zr, xs, xr, ts, tr, bs, br, cs, cr, ys, yr, fs, fr,
):
    ka, h, y = lax.axis_index("ka"), lax.axis_index("tr"), lax.axis_index("tc")
    x, z, c = ka // 8, (ka // 2) % 4, ka % 2
    xc = x * 2 + c
    arrays = (less, great, screen)

    def at(xx, zz, cc):
        return xx * 8 + zz * 2 + cc

    zpeers = [3 - z, (z + 2) % 4, z + 1 - 2 * (z % 2)]
    xpeers = [
        ((x + 2) % 4, c), ((x + 2) % 4, 1 - c), ((x + 1) % 4, c), ((x + 3) % 4, 1 - c),
        ((x + 1) % 4, 1 - c), ((x + 3) % 4, c), (x, 1 - c),
    ]
    up, down = (y + 1) % 4, (y + 3) % 4

    def remote(src, dst, send, recv, peer):
        copy = pltpu.make_async_remote_copy(
            src_ref=src, dst_ref=dst, send_sem=send, recv_sem=recv, device_id=peer, device_id_type=MESH
        )
        copy.start()

    def done(ref, sem):
        pltpu.make_async_copy(ref, ref, sem).wait()

    def three(m, a=0):
        return zbuf.at[m, a, pl.ds(0, 3)]

    def four(m):
        return zbuf.at[m, 0]

    def eight(m):
        return zbuf.at[m, pl.ds(0, 2)]

    def seven(m, a=0):
        return tile.at[m, a, pl.ds(0, 7)]

    def rows(start, size):
        return pl.ds(pl.multiple_of(start, 8), size)

    def zrows(m, zz):
        return rows((m // 2) * CROWS + zz * ZROWS, ZROWS)

    def cols(m):
        return pl.ds((m % 2) * CCOLS, CCOLS)

    def xrows(index):
        return rows(index * TROWS, TROWS)

    own = [
        [
            pltpu.make_async_copy(arrays[a].at[:, 0, zrows(m, z), cols(m)], zbuf.at[m, a, z], own_sem.at[1 + 3 * m + a])
            for a in range(3)
        ]
        for m in range(CHUNKS)
    ]
    load = pltpu.make_async_copy(less.at[:, 0], gloc, own_sem.at[0])

    def send_z(m, a):
        for i, zz in enumerate(zpeers):
            remote(
                arrays[a].at[:, 0, zrows(m, zz), cols(m)], zbuf.at[m, a, z],
                zs.at[m, a], zr.at[m, a], (at(x, zz, c), h, y),
            )

    def send_x(m, a):
        own[m][a].wait()
        done(three(m, a), zr.at[m, a])
        for i, (xx, cc) in enumerate(xpeers):
            remote(
                zbuf.at[m, a, :, :, xrows(xx * 2 + cc), :], tile.at[m, a, xc],
                xs.at[m, a], xr.at[m, a], (at(xx, z, cc), h, y),
            )
        tile[m, a, xc] = zbuf[m, a, :, :, xrows(xc), :]

    def share_less(m, places):
        for i, zz in enumerate([z] + zpeers):
            if i not in places:
                continue
            remote(
                zbuf.at[m, 0, zz], grem.at[:, zrows(m, z), cols(m)],
                ts.at[m], tr.at[m], (at(x, zz, c), 1 - h, y),
            )

    def wait_less(m):
        done(four(m), tr.at[m])

    def transform(m):
        for a in range(3):
            done(seven(m, a), xr.at[m, a])
        for a in range(3):
            for k2 in range(8):
                j, cc = k2 // 2, k2 % 2
                values = [(tile[m, a, 2 * xx + cc, j, 0], tile[m, a, 2 * xx + cc, j, 1]) for xx in range(4)]
                for r1, value in enumerate(dft(values, 1)):
                    mid[a, r1, k2, 0], mid[a, r1, k2, 1] = cmul(value, k2 * r1)
        for r1 in range(4):
            sides = [dft([(mid[a, r1, k2, 0], mid[a, r1, k2, 1]) for k2 in range(8)], 1) for a in range(3)]
            out = []
            for (lr, li), (gr, gi), (wr, wi) in zip(*sides):
                ir = OUTER * wr + (OUTER * INNER) * (lr * gi - li * gr)
                ii = OUTER * wi + (OUTER * INNER) * (lr * gr + li * gi)
                out.append((-(lr * ii + li * ir), lr * ir - li * ii))
            for k2, value in enumerate(dft(out, -1)):
                mid2[r1, k2, 0], mid2[r1, k2, 1] = cmul(value, -k2 * r1)
        for k2 in range(8):
            j, cc = k2 // 2, k2 % 2
            for xx, value in enumerate(dft([(mid2[r1, k2, 0], mid2[r1, k2, 1]) for r1 in range(4)], -1)):
                sig[m, 2 * xx + cc, j, 0], sig[m, 2 * xx + cc, j, 1] = value
        for i, (xx, cc) in enumerate(xpeers):
            remote(
                sig.at[m, xx * 2 + cc], back.at[m, :, :, xrows(xc), :], bs.at[m], br.at[m], (at(xx, z, cc), h, y)
            )
        back[m, :, :, xrows(xc), :] = sig[m, xc]

    def back_z(m):
        done(seven(m), br.at[m])
        for i, zz in enumerate(zpeers):
            remote(back.at[m, zz], sigma.at[y, m % 2, :, zrows(m, z), :], cs.at[m], cr.at[m, i], (at(x, zz, c), h, y))
        sigma[y, m % 2, :, zrows(m, z), :] = back[m, z]

    pieces = [z] + zpeers

    def piece(yy, m, i):
        return sigma.at[yy, m % 2, :, zrows(m, pieces[i]), :]

    def spread_y(m, i):
        if i > 0:
            done(piece(y, m, i), cr.at[m, i - 1])
        remote(piece(y, m, i), piece(y, m, i), ys.at[m], yr.at[m, i, 0], (ka, h, up))
        remote(piece(y, m, i), piece(y, m, i), ys.at[m], yr.at[m, i, 1], (ka, h, down))

    def relay_y(m, i):
        done(piece(down, m, i), yr.at[m, i, 0])
        if i % 2 == 0:
            remote(piece(down, m, i), piece(down, m, i), fs.at[m], fr.at[m], (ka, h, up))
        done(piece(up, m, i), yr.at[m, i, 1])
        if i % 2 == 1:
            remote(piece(up, m, i), piece(up, m, i), fs.at[m], fr.at[m], (ka, h, down))

    def wait_y(m):
        done(four(m), fr.at[m])

    def prepare(source, part, blocks):
        for s in blocks:
            re, im = source[0, s * 128:(s + 1) * 128, :], source[1, s * 128:(s + 1) * 128, :]
            for value, places in ((re, ((0, 0), (128, 256))), (im, ((0, 256),)), (-im, ((128, 0),))):
                high, low = split(value)
                for row, col in places:
                    ghigh[part * 4 + s, row:row + 128, col:col + 256] = high
                    glow[part * 4 + s, row:row + 128, col:col + 256] = low

    def multiply(m, part, first, last):
        def block(s, carry):
            multiply_one(m, part * 2 + s)
            return carry

        lax.fori_loop(first, last, block, 0)

    def multiply_one(m, yy):
        span = pl.ds((m // 2) * CROWS, CROWS)
        left = jnp.concatenate([sigma[yy, m % 2, 0, span, :], sigma[yy, m % 2, 1, span, :]], axis=1)
        high, low = split(left)
        index = yy * 2 + m % 2
        total = jnp.dot(high, ghigh[index], preferred_element_type=jnp.float32)
        total += jnp.dot(high, glow[index], preferred_element_type=jnp.float32)
        total += jnp.dot(low, ghigh[index], preferred_element_type=jnp.float32)
        for ri in range(2):
            product[ri, 0, span, :] += total[:, ri * 256:(ri + 1) * 256]

    def finish(n):
        del n

    barrier = pltpu.get_barrier_semaphore()
    peers = [(at(x, zz, c), h, y) for zz in zpeers]
    peers += [(at(x, zz, c), 1 - h, y) for zz in range(4)]
    peers += [(at(xx, z, cc), h, y) for xx, cc in xpeers]
    peers += [(ka, h, up), (ka, h, down)]
    for peer in peers:
        pl.semaphore_signal(barrier, inc=1, device_id=peer, device_id_type=MESH)
    for a in range(3):
        for m in range(CHUNKS):
            own[m][a].start()
    load.start()
    pl.semaphore_wait(barrier, len(peers))

    send_z(0, 0)
    send_z(0, 1)
    product[...] = jnp.zeros_like(product)
    load.wait()
    prepare(gloc, h, range(4))
    send_z(0, 2)
    send_x(0, 0)
    send_z(1, 0)
    send_z(1, 1)
    share_less(0, (1, 2))
    send_x(0, 1)
    send_z(1, 2)
    send_x(0, 2)
    send_z(2, 0)
    send_x(1, 0)
    share_less(1, (1, 2))
    send_z(2, 1)
    transform(0)
    send_x(1, 1)
    send_z(2, 2)
    back_z(0)
    send_x(1, 2)
    send_z(3, 0)
    send_x(2, 0)
    share_less(2, (1, 2))
    send_z(3, 1)
    transform(1)
    send_x(2, 1)
    send_z(3, 2)
    back_z(1)
    send_x(2, 2)
    spread_y(0, 0)
    spread_y(0, 3)
    spread_y(0, 1)
    spread_y(0, 2)
    send_x(3, 0)
    share_less(3, (1, 2))
    share_less(0, (0, 3))
    transform(2)
    send_x(3, 1)
    relay_y(0, 0)
    relay_y(0, 3)
    relay_y(0, 1)
    relay_y(0, 2)
    back_z(2)
    send_x(3, 2)
    share_less(1, (0, 3))
    transform(3)
    spread_y(1, 0)
    spread_y(1, 3)
    spread_y(1, 1)
    spread_y(1, 2)
    wait_y(0)
    multiply(0, h, 0, 2)
    back_z(3)
    spread_y(2, 0)
    relay_y(1, 0)
    relay_y(1, 3)
    spread_y(2, 3)
    relay_y(1, 1)
    relay_y(1, 2)
    spread_y(2, 1)
    spread_y(2, 2)
    spread_y(3, 0)
    relay_y(2, 0)
    relay_y(2, 3)
    spread_y(3, 3)
    relay_y(2, 1)
    spread_y(3, 1)
    share_less(2, (0, 3))
    share_less(3, (0, 3))
    relay_y(2, 2)
    spread_y(3, 2)
    wait_y(1)
    multiply(1, h, 0, 2)
    wait_less(0)
    wait_less(1)
    prepare(grem, 1 - h, range(0, 2))
    multiply(0, 1 - h, 0, 1)
    multiply(1, 1 - h, 0, 1)
    relay_y(3, 0)
    relay_y(3, 3)
    relay_y(3, 1)
    relay_y(3, 2)
    wait_y(2)
    multiply(2, h, 0, 2)
    multiply(2, 1 - h, 0, 1)
    wait_less(2)
    wait_less(3)
    prepare(grem, 1 - h, range(2, 4))
    multiply(0, 1 - h, 1, 2)
    multiply(1, 1 - h, 1, 2)
    finish(0)
    multiply(2, 1 - h, 1, 2)
    multiply_one(3, y)
    multiply_one(3, up)
    multiply_one(3, down)
    wait_y(3)
    multiply_one(3, (y + 2) % 4)
    finish(1)
    for m in range(CHUNKS):
        for a in range(3):
            done(three(m, a), zs.at[m, a])
            done(seven(m, a), xs.at[m, a])
        done(four(m), ts.at[m])
        done(seven(m), bs.at[m])
        done(three(m), cs.at[m])
        done(eight(m), ys.at[m])
        done(four(m), fs.at[m])


def body(green_less, green_great, screened):
    dma = pltpu.SemaphoreType.DMA
    block = jax.ShapeDtypeStruct(green_less.shape, jnp.float32)
    f32, bf16 = jnp.float32, jnp.bfloat16
    product = pl.pallas_call(
        kernel,
        out_shape=block,
        in_specs=[pl.BlockSpec(memory_space=pl.ANY)] * 3,
        out_specs=pl.BlockSpec(memory_space=pltpu.VMEM),
        scratch_shapes=[
            pltpu.VMEM((CHUNKS, 3, 4, 2, ZROWS, CCOLS), f32),
            pltpu.VMEM((CHUNKS, 3, 8, 4, 2, TROWS, CCOLS), f32),
            pltpu.VMEM((3, 4, 8, 2, TROWS, CCOLS), f32),
            pltpu.VMEM((4, 8, 2, TROWS, CCOLS), f32),
            pltpu.VMEM((CHUNKS, 8, 4, 2, TROWS, CCOLS), f32),
            pltpu.VMEM((CHUNKS, 4, 2, ZROWS, CCOLS), f32),
            pltpu.VMEM((4, 2, 2, ROWS, CCOLS), f32),
            pltpu.VMEM((2, ROWS, COLS), f32),
            pltpu.VMEM((2, ROWS, COLS), f32),
            pltpu.VMEM((8, 256, 512), bf16),
            pltpu.VMEM((8, 256, 512), bf16),
            dma((1 + 3 * CHUNKS,)),
            dma((CHUNKS, 3)), dma((CHUNKS, 3)),
            dma((CHUNKS, 3)), dma((CHUNKS, 3)),
            dma((CHUNKS,)), dma((CHUNKS,)),
            dma((CHUNKS,)), dma((CHUNKS,)),
            dma((CHUNKS,)), dma((CHUNKS, 3)),
            dma((CHUNKS,)), dma((CHUNKS, 4, 2)),
            dma((CHUNKS,)), dma((CHUNKS,)),
        ],
        compiler_params=pltpu.CompilerParams(collective_id=0, has_side_effects=True, vmem_limit_bytes=52 << 20),
        name="collide",
    )(green_less, green_great, screened)
    collision = product * NORM
    return collision, green_less + collision


def solution(mesh):
    spec = P(None, "ka", "tr", "tc")
    return jax.shard_map(body, mesh=mesh, in_specs=(spec,) * 3, out_specs=(spec,) * 2, check_vma=False)
```

```python
import functools
import math

import jax
import jax.numpy as jnp
from jax import lax
from jax.experimental import pallas as pl
from jax.experimental.pallas import tpu as pltpu
from jax.sharding import PartitionSpec as P

MESH = pl.DeviceIdType.MESH
ROWS = 512
COLS = 256
CHUNKS = 4
CROWS = 256
CCOLS = 128
ZROWS = CROWS // 4
TROWS = ZROWS // 8
INNER = 32.0 ** -0.5
OUTER = 1.0 / (32.0 * math.sqrt(32.0))
NORM = 1.0 / 32.0


def cmul(value, turns):
    turns = turns % 32
    re, im = value
    if turns == 0:
        return value
    if turns == 8:
        return -im, re
    if turns == 16:
        return -re, -im
    if turns == 24:
        return im, -re
    cos, sin = math.cos(2 * math.pi * turns / 32), math.sin(2 * math.pi * turns / 32)
    if turns % 8 == 4:
        root = math.sqrt(0.5)
        plus, minus = (re + im) * root, (re - im) * root
        return {4: (minus, plus), 12: (-plus, minus), 20: (-minus, -plus), 28: (plus, -minus)}[turns]
    return re * cos - im * sin, re * sin + im * cos


def cadd(a, b):
    return a[0] + b[0], a[1] + b[1]


def csub(a, b):
    return a[0] - b[0], a[1] - b[1]


def dft(values, sign):
    size = len(values)
    if size == 1:
        return values
    even, odd = dft(values[0::2], sign), dft(values[1::2], sign)
    step = 32 // size
    low, high = [], []
    for m in range(size // 2):
        turned = cmul(odd[m], sign * step * m)
        low.append(cadd(even[m], turned))
        high.append(csub(even[m], turned))
    return low + high


def split(value):
    high = value.astype(jnp.bfloat16)
    return high, (value - high.astype(jnp.float32)).astype(jnp.bfloat16)


def kernel(
    less, great, screen, product,
    zbuf, tile, mid, mid2, sig, back, sigma, gloc, grem, ghigh, glow,
    own_sem, zs, zr, xr, tr, br, cr, yr, yn, fr,
):
    ka, h, y = lax.axis_index("ka"), lax.axis_index("tr"), lax.axis_index("tc")
    x, z, c = ka // 8, (ka // 2) % 4, ka % 2
    xc = x * 2 + c
    arrays = (less, great, screen)

    def at(xx, zz, cc):
        return xx * 8 + zz * 2 + cc

    zpeers = [3 - z, (z + 2) % 4, z + 1 - 2 * (z % 2)]
    xpeers = [
        ((x + 2) % 4, c), ((x + 2) % 4, 1 - c), ((x + 1) % 4, c), ((x + 3) % 4, 1 - c),
        ((x + 1) % 4, 1 - c), ((x + 3) % 4, c), (x, 1 - c),
    ]
    up, down = (y + 1) % 4, (y + 3) % 4

    def remote(src, dst, send, recv, peer):
        copy = pltpu.make_async_remote_copy(
            src_ref=src, dst_ref=dst, send_sem=send, recv_sem=recv, device_id=peer, device_id_type=MESH
        )
        copy.start()

    def done(ref, sem):
        pltpu.make_async_copy(ref, ref, sem).wait()

    def three(m, a=0):
        return zbuf.at[m, a, pl.ds(0, 3)]

    def four(m):
        return zbuf.at[m, 0]

    def eight(m):
        return zbuf.at[m, pl.ds(0, 2)]

    def seven(m, a=0):
        return tile.at[m, a, pl.ds(0, 7)]

    def rows(start, size):
        return pl.ds(pl.multiple_of(start, 8), size)

    def zrows(m, zz):
        return rows((m // 2) * CROWS + zz * ZROWS, ZROWS)

    def cols(m):
        return pl.ds((m % 2) * CCOLS, CCOLS)

    def xrows(index):
        return rows(index * TROWS, TROWS)

    own = [
        [
            pltpu.make_async_copy(arrays[a].at[:, 0, zrows(m, z), cols(m)], zbuf.at[m, a, z], own_sem.at[1 + a])
            for a in range(3)
        ]
        for m in range(CHUNKS)
    ]
    load = pltpu.make_async_copy(less.at[:, 0], gloc, own_sem.at[0])

    def send_z(m, a):
        for i, zz in enumerate(zpeers):
            remote(
                arrays[a].at[:, 0, zrows(m, zz), cols(m)], zbuf.at[m, a, z],
                zs.at[0], zr.at[m, a], (at(x, zz, c), h, y),
            )

    def send_x(m, a):
        if m == 0:
            done(four(0), own_sem.at[1 + a])
        done(three(m, a), zr.at[m, a])
        for i, (xx, cc) in enumerate(xpeers):
            remote(
                zbuf.at[m, a, :, :, xrows(xx * 2 + cc), :], tile.at[m, a, xc],
                zs.at[1], xr.at[m, a], (at(xx, z, cc), h, y),
            )
        tile[m, a, xc] = zbuf[m, a, :, :, xrows(xc), :]

    def share_less(m, places):
        for i, zz in enumerate([z] + zpeers):
            if i not in places:
                continue
            remote(
                zbuf.at[m, 0, zz], grem.at[:, zrows(m, z), cols(m)],
                zs.at[2], tr.at[m], (at(x, zz, c), 1 - h, y),
            )

    def wait_less(m):
        done(four(m), tr.at[m])

    def transform(m):
        for a in range(3):
            done(seven(m, a), xr.at[m, a])
        for a in range(3):
            for k2 in range(8):
                j, cc = k2 // 2, k2 % 2
                values = [(tile[m, a, 2 * xx + cc, j, 0], tile[m, a, 2 * xx + cc, j, 1]) for xx in range(4)]
                for r1, value in enumerate(dft(values, 1)):
                    mid[a, r1, k2, 0], mid[a, r1, k2, 1] = cmul(value, k2 * r1)
        for r1 in range(4):
            sides = [dft([(mid[a, r1, k2, 0], mid[a, r1, k2, 1]) for k2 in range(8)], 1) for a in range(3)]
            out = []
            for (lr, li), (gr, gi), (wr, wi) in zip(*sides):
                ir = OUTER * wr + (OUTER * INNER) * (lr * gi - li * gr)
                ii = OUTER * wi + (OUTER * INNER) * (lr * gr + li * gi)
                out.append((-(lr * ii + li * ir), lr * ir - li * ii))
            for k2, value in enumerate(dft(out, -1)):
                mid2[r1, k2, 0], mid2[r1, k2, 1] = cmul(value, -k2 * r1)
        for k2 in range(8):
            j, cc = k2 // 2, k2 % 2
            for xx, value in enumerate(dft([(mid2[r1, k2, 0], mid2[r1, k2, 1]) for r1 in range(4)], -1)):
                sig[m, 2 * xx + cc, j, 0], sig[m, 2 * xx + cc, j, 1] = value
        for i, (xx, cc) in enumerate(xpeers):
            remote(
                sig.at[m, xx * 2 + cc], back.at[m, :, :, xrows(xc), :], zs.at[3], br.at[m], (at(xx, z, cc), h, y)
            )
        back[m, :, :, xrows(xc), :] = sig[m, xc]

    def back_z(m):
        done(seven(m), br.at[m])
        for i, zz in enumerate(zpeers):
            remote(back.at[m, zz], sigma.at[y, m % 2, :, zrows(m, z), :], zs.at[4], cr.at[m, i], (at(x, zz, c), h, y))
        sigma[y, m % 2, :, zrows(m, z), :] = back[m, z]

    pieces = [z] + zpeers

    def piece(yy, m, i):
        return sigma.at[yy, m % 2, :, zrows(m, pieces[i]), :]

    def spread_y(m, i):
        if i > 0:
            done(piece(y, m, i), cr.at[m, i - 1])
        ups = (yr.at[m, i], yn.at[m])
        for peer, sem in (((ka, h, up), ups[i % 2]), ((ka, h, down), ups[1 - i % 2])):
            remote(piece(y, m, i), piece(y, m, i), zs.at[5], sem, peer)

    def relay_y(m, i):
        source, target = ((down, up), (up, down))[i % 2]
        done(piece(source, m, i), yr.at[m, i])
        remote(piece(source, m, i), piece(source, m, i), zs.at[6], fr.at[m], (ka, h, target))

    def wait_near(m):
        done(four(m), yn.at[m])

    def wait_y(m):
        done(four(m), fr.at[m])

    def prepare(source, part, blocks):
        for s in blocks:
            re, im = source[0, s * 128:(s + 1) * 128, :], source[1, s * 128:(s + 1) * 128, :]
            for value, places in ((re, ((0, 0), (128, 256))), (im, ((0, 256),)), (-im, ((128, 0),))):
                high, low = split(value)
                for row, col in places:
                    ghigh[part * 4 + s, row:row + 128, col:col + 256] = high
                    glow[part * 4 + s, row:row + 128, col:col + 256] = low

    def multiply(m, part, first, last):
        def block(s, carry):
            multiply_one(m, part * 2 + s)
            return carry

        lax.fori_loop(first, last, block, 0)

    def multiply_one(m, yy):
        span = pl.ds((m // 2) * CROWS, CROWS)
        left = jnp.concatenate([sigma[yy, m % 2, 0, span, :], sigma[yy, m % 2, 1, span, :]], axis=1)
        high, low = split(left)
        index = yy * 2 + m % 2
        total = jnp.dot(high, ghigh[index], preferred_element_type=jnp.float32)
        total += jnp.dot(high, glow[index], preferred_element_type=jnp.float32)
        total += jnp.dot(low, ghigh[index], preferred_element_type=jnp.float32)
        for ri in range(2):
            product[ri, 0, span, :] += total[:, ri * 256:(ri + 1) * 256]

    barrier = pltpu.get_barrier_semaphore()
    peers = [(at(x, zz, c), h, y) for zz in zpeers]
    peers += [(at(x, zz, c), 1 - h, y) for zz in range(4)]
    peers += [(at(xx, z, cc), h, y) for xx, cc in xpeers]
    peers += [(ka, h, up), (ka, h, down)]
    for peer in peers:
        pl.semaphore_signal(barrier, inc=1, device_id=peer, device_id_type=MESH)
    for a in range(3):
        for m in range(CHUNKS):
            own[m][a].start()
    load.start()
    pl.semaphore_wait(barrier, len(peers))

    send_z(0, 0)
    send_z(0, 1)
    product[...] = jnp.zeros_like(product)
    load.wait()
    prepare(gloc, h, range(4))
    send_z(0, 2)
    send_x(0, 0)
    send_z(1, 0)
    send_z(1, 1)
    share_less(0, (1, 2))
    send_x(0, 1)
    send_z(1, 2)
    send_x(0, 2)
    send_z(2, 0)
    send_x(1, 0)
    share_less(1, (1, 2))
    send_z(2, 1)
    transform(0)
    send_x(1, 1)
    send_z(2, 2)
    back_z(0)
    send_x(1, 2)
    send_z(3, 0)
    send_x(2, 0)
    share_less(2, (1, 2))
    send_z(3, 1)
    transform(1)
    send_x(2, 1)
    send_z(3, 2)
    back_z(1)
    send_x(2, 2)
    spread_y(0, 0)
    spread_y(0, 3)
    spread_y(0, 1)
    spread_y(0, 2)
    send_x(3, 0)
    share_less(3, (1, 2))
    share_less(0, (0, 3))
    transform(2)
    send_x(3, 1)
    relay_y(0, 0)
    relay_y(0, 3)
    relay_y(0, 1)
    relay_y(0, 2)
    back_z(2)
    send_x(3, 2)
    share_less(1, (0, 3))
    transform(3)
    spread_y(1, 0)
    spread_y(1, 3)
    spread_y(1, 1)
    spread_y(1, 2)
    wait_near(0)
    wait_y(0)
    multiply(0, h, 0, 2)
    back_z(3)
    spread_y(2, 0)
    relay_y(1, 0)
    relay_y(1, 3)
    spread_y(2, 3)
    relay_y(1, 1)
    relay_y(1, 2)
    spread_y(2, 1)
    spread_y(2, 2)
    spread_y(3, 0)
    relay_y(2, 0)
    relay_y(2, 3)
    spread_y(3, 3)
    relay_y(2, 1)
    spread_y(3, 1)
    share_less(2, (0, 3))
    share_less(3, (0, 3))
    relay_y(2, 2)
    spread_y(3, 2)
    wait_near(1)
    wait_y(1)
    multiply(1, h, 0, 2)
    wait_less(0)
    wait_less(1)
    prepare(grem, 1 - h, range(0, 2))
    multiply(0, 1 - h, 0, 1)
    multiply(1, 1 - h, 0, 1)
    relay_y(3, 0)
    relay_y(3, 3)
    relay_y(3, 1)
    relay_y(3, 2)
    wait_near(2)
    wait_y(2)
    multiply(2, h, 0, 2)
    multiply(2, 1 - h, 0, 1)
    wait_less(2)
    wait_less(3)
    prepare(grem, 1 - h, range(2, 4))
    multiply(0, 1 - h, 1, 2)
    multiply(1, 1 - h, 1, 2)
    multiply(2, 1 - h, 1, 2)
    wait_near(3)
    multiply_one(3, y)
    multiply_one(3, up)
    multiply_one(3, down)
    wait_y(3)
    multiply_one(3, (y + 2) % 4)
    done(zbuf.at[:, :, pl.ds(0, 3)], zs.at[0])
    done(tile.at[:, :, pl.ds(0, 7)], zs.at[1])
    done(zbuf.at[:, 0], zs.at[2])
    done(tile.at[:, 0, pl.ds(0, 7)], zs.at[3])
    done(zbuf.at[:, 0, pl.ds(0, 3)], zs.at[4])
    done(zbuf.at[:, pl.ds(0, 2)], zs.at[5])
    done(zbuf.at[:, 0], zs.at[6])


def body(green_less, green_great, screened):
    dma = pltpu.SemaphoreType.DMA
    block = jax.ShapeDtypeStruct(green_less.shape, jnp.float32)
    f32, bf16 = jnp.float32, jnp.bfloat16
    product = pl.pallas_call(
        kernel,
        out_shape=block,
        in_specs=[pl.BlockSpec(memory_space=pl.ANY)] * 3,
        out_specs=pl.BlockSpec(memory_space=pltpu.VMEM),
        scratch_shapes=[
            pltpu.VMEM((CHUNKS, 3, 4, 2, ZROWS, CCOLS), f32),
            pltpu.VMEM((CHUNKS, 3, 8, 4, 2, TROWS, CCOLS), f32),
            pltpu.VMEM((3, 4, 8, 2, TROWS, CCOLS), f32),
            pltpu.VMEM((4, 8, 2, TROWS, CCOLS), f32),
            pltpu.VMEM((CHUNKS, 8, 4, 2, TROWS, CCOLS), f32),
            pltpu.VMEM((CHUNKS, 4, 2, ZROWS, CCOLS), f32),
            pltpu.VMEM((4, 2, 2, ROWS, CCOLS), f32),
            pltpu.VMEM((2, ROWS, COLS), f32),
            pltpu.VMEM((2, ROWS, COLS), f32),
            pltpu.VMEM((8, 256, 512), bf16),
            pltpu.VMEM((8, 256, 512), bf16),
            dma((4,)), dma((7,)),
            dma((CHUNKS, 3)), dma((CHUNKS, 3)),
            dma((CHUNKS,)), dma((CHUNKS,)), dma((CHUNKS, 3)),
            dma((CHUNKS, 4)), dma((CHUNKS,)), dma((CHUNKS,)),
        ],
        compiler_params=pltpu.CompilerParams(collective_id=0, has_side_effects=True, vmem_limit_bytes=52 << 20),
        name="collide",
    )(green_less, green_great, screened)
    collision = product * NORM
    return collision, green_less + collision


def solution(mesh):
    spec = P(None, "ka", "tr", "tc")
    return jax.shard_map(body, mesh=mesh, in_specs=(spec,) * 3, out_specs=(spec,) * 2, check_vma=False)
```

```python
import functools
import math

import jax
import jax.numpy as jnp
from jax import lax
from jax.experimental import pallas as pl
from jax.experimental.pallas import tpu as pltpu
from jax.sharding import PartitionSpec as P

MESH = pl.DeviceIdType.MESH
ROWS = 512
COLS = 256
CHUNKS = 4
CROWS = 256
CCOLS = 128
ZROWS = CROWS // 4
TROWS = ZROWS // 8
INNER = 32.0 ** -0.5
OUTER = 1.0 / (32.0 * math.sqrt(32.0))
NORM = 1.0 / 32.0


def cmul(value, turns):
    turns = turns % 32
    re, im = value
    if turns == 0:
        return value
    if turns == 8:
        return -im, re
    if turns == 16:
        return -re, -im
    if turns == 24:
        return im, -re
    cos, sin = math.cos(2 * math.pi * turns / 32), math.sin(2 * math.pi * turns / 32)
    if turns % 8 == 4:
        root = math.sqrt(0.5)
        plus, minus = (re + im) * root, (re - im) * root
        return {4: (minus, plus), 12: (-plus, minus), 20: (-minus, -plus), 28: (plus, -minus)}[turns]
    return re * cos - im * sin, re * sin + im * cos


def cadd(a, b):
    return a[0] + b[0], a[1] + b[1]


def csub(a, b):
    return a[0] - b[0], a[1] - b[1]


def dft(values, sign):
    size = len(values)
    if size == 1:
        return values
    even, odd = dft(values[0::2], sign), dft(values[1::2], sign)
    step = 32 // size
    low, high = [], []
    for m in range(size // 2):
        turned = cmul(odd[m], sign * step * m)
        low.append(cadd(even[m], turned))
        high.append(csub(even[m], turned))
    return low + high


def split(value):
    high = value.astype(jnp.bfloat16)
    return high, (value - high.astype(jnp.float32)).astype(jnp.bfloat16)


def kernel(
    less, great, screen, product,
    zbuf, tile, mid, mid2, sig, back, sigma, gloc, grem, ghigh, glow,
    own_sem, zs, zr, xr, tr, br, cr, yr, yn, fr,
):
    ka, h, y = lax.axis_index("ka"), lax.axis_index("tr"), lax.axis_index("tc")
    x, z, c = ka // 8, (ka // 2) % 4, ka % 2
    xc = x * 2 + c
    arrays = (less, great, screen)

    def at(xx, zz, cc):
        return xx * 8 + zz * 2 + cc

    zpeers = [(z + 2) % 4, 3 - z, z + 1 - 2 * (z % 2)]
    xpeers = [
        ((x + 2) % 4, c), ((x + 2) % 4, 1 - c), ((x + 1) % 4, c), ((x + 3) % 4, 1 - c),
        ((x + 1) % 4, 1 - c), ((x + 3) % 4, c), (x, 1 - c),
    ]
    up, down = (y + 1) % 4, (y + 3) % 4

    def remote(src, dst, send, recv, peer):
        copy = pltpu.make_async_remote_copy(
            src_ref=src, dst_ref=dst, send_sem=send, recv_sem=recv, device_id=peer, device_id_type=MESH
        )
        copy.start()

    def done(ref, sem):
        pltpu.make_async_copy(ref, ref, sem).wait()

    def three(m, a=0):
        return zbuf.at[m, a, pl.ds(0, 3)]

    def four(m):
        return zbuf.at[m, 0]

    def eight(m):
        return zbuf.at[m, pl.ds(0, 2)]

    def seven(m, a=0):
        return tile.at[m, a, pl.ds(0, 7)]

    def rows(start, size):
        return pl.ds(pl.multiple_of(start, 8), size)

    def zrows(m, zz):
        return rows((m // 2) * CROWS + zz * ZROWS, ZROWS)

    def cols(m):
        return pl.ds((m % 2) * CCOLS, CCOLS)

    def xrows(index):
        return rows(index * TROWS, TROWS)

    own = [
        [
            pltpu.make_async_copy(arrays[a].at[:, 0, zrows(m, z), cols(m)], zbuf.at[m, a, z], own_sem.at[1 + a])
            for a in range(3)
        ]
        for m in range(CHUNKS)
    ]
    load = pltpu.make_async_copy(less.at[:, 0], gloc, own_sem.at[0])

    def send_z(m, a):
        for i, zz in enumerate(zpeers):
            remote(
                arrays[a].at[:, 0, zrows(m, zz), cols(m)], zbuf.at[m, a, z],
                zs.at[0], zr.at[m, a], (at(x, zz, c), h, y),
            )

    def send_x(m, a):
        if m == 0:
            done(four(0), own_sem.at[1 + a])
        done(three(m, a), zr.at[m, a])
        for i, (xx, cc) in enumerate(xpeers):
            remote(
                zbuf.at[m, a, :, :, xrows(xx * 2 + cc), :], tile.at[m, a, xc],
                zs.at[1], xr.at[m, a], (at(xx, z, cc), h, y),
            )
        tile[m, a, xc] = zbuf[m, a, :, :, xrows(xc), :]

    def share_less(m, places):
        for i, zz in enumerate([z] + zpeers):
            if i not in places:
                continue
            remote(
                zbuf.at[m, 0, zz], grem.at[:, zrows(m, z), cols(m)],
                zs.at[2], tr.at[m], (at(x, zz, c), 1 - h, y),
            )

    def wait_less(m):
        done(four(m), tr.at[m])

    def transform(m):
        for a in range(3):
            done(seven(m, a), xr.at[m, a])
        for a in range(3):
            for k2 in range(8):
                j, cc = k2 // 2, k2 % 2
                values = [(tile[m, a, 2 * xx + cc, j, 0], tile[m, a, 2 * xx + cc, j, 1]) for xx in range(4)]
                for r1, value in enumerate(dft(values, 1)):
                    mid[a, r1, k2, 0], mid[a, r1, k2, 1] = cmul(value, k2 * r1)
        for r1 in range(4):
            sides = [dft([(mid[a, r1, k2, 0], mid[a, r1, k2, 1]) for k2 in range(8)], 1) for a in range(3)]
            out = []
            for (lr, li), (gr, gi), (wr, wi) in zip(*sides):
                ir = OUTER * wr + (OUTER * INNER) * (lr * gi - li * gr)
                ii = OUTER * wi + (OUTER * INNER) * (lr * gr + li * gi)
                out.append((-(lr * ii + li * ir), lr * ir - li * ii))
            for k2, value in enumerate(dft(out, -1)):
                mid2[r1, k2, 0], mid2[r1, k2, 1] = cmul(value, -k2 * r1)
        for k2 in range(8):
            j, cc = k2 // 2, k2 % 2
            for xx, value in enumerate(dft([(mid2[r1, k2, 0], mid2[r1, k2, 1]) for r1 in range(4)], -1)):
                sig[m, 2 * xx + cc, j, 0], sig[m, 2 * xx + cc, j, 1] = value
        for i, (xx, cc) in enumerate(xpeers):
            remote(
                sig.at[m, xx * 2 + cc], back.at[m, :, :, xrows(xc), :], zs.at[3], br.at[m], (at(xx, z, cc), h, y)
            )
        back[m, :, :, xrows(xc), :] = sig[m, xc]

    def back_z(m):
        done(seven(m), br.at[m])
        for i, zz in enumerate(zpeers):
            remote(back.at[m, zz], sigma.at[y, m % 2, :, zrows(m, z), :], zs.at[4], cr.at[m, i], (at(x, zz, c), h, y))
        sigma[y, m % 2, :, zrows(m, z), :] = back[m, z]

    pieces = [z] + zpeers

    def piece(yy, m, i):
        return sigma.at[yy, m % 2, :, zrows(m, pieces[i]), :]

    def spread_y(m, i):
        if i > 0:
            done(piece(y, m, i), cr.at[m, i - 1])
        ups = (yr.at[m, i], yn.at[m])
        for peer, sem in (((ka, h, up), ups[i % 2]), ((ka, h, down), ups[1 - i % 2])):
            remote(piece(y, m, i), piece(y, m, i), zs.at[5], sem, peer)

    def relay_y(m, i):
        source, target = ((down, up), (up, down))[i % 2]
        done(piece(source, m, i), yr.at[m, i])
        remote(piece(source, m, i), piece(source, m, i), zs.at[6], fr.at[m], (ka, h, target))

    def wait_near(m):
        done(four(m), yn.at[m])

    def wait_y(m):
        done(four(m), fr.at[m])

    def prepare(source, part, blocks):
        for s in blocks:
            re, im = source[0, s * 128:(s + 1) * 128, :], source[1, s * 128:(s + 1) * 128, :]
            for value, places in ((re, ((0, 0), (128, 256))), (im, ((0, 256),)), (-im, ((128, 0),))):
                high, low = split(value)
                for row, col in places:
                    ghigh[part * 4 + s, row:row + 128, col:col + 256] = high
                    glow[part * 4 + s, row:row + 128, col:col + 256] = low

    def multiply(m, part, first, last):
        def block(s, carry):
            multiply_one(m, part * 2 + s)
            return carry

        lax.fori_loop(first, last, block, 0)

    def multiply_one(m, yy):
        span = pl.ds((m // 2) * CROWS, CROWS)
        left = jnp.concatenate([sigma[yy, m % 2, 0, span, :], sigma[yy, m % 2, 1, span, :]], axis=1)
        high, low = split(left)
        index = yy * 2 + m % 2
        total = jnp.dot(high, ghigh[index], preferred_element_type=jnp.float32)
        total += jnp.dot(high, glow[index], preferred_element_type=jnp.float32)
        total += jnp.dot(low, ghigh[index], preferred_element_type=jnp.float32)
        for ri in range(2):
            product[ri, 0, span, :] += total[:, ri * 256:(ri + 1) * 256]

    barrier = pltpu.get_barrier_semaphore()
    peers = [(at(x, zz, c), h, y) for zz in zpeers]
    peers += [(at(x, zz, c), 1 - h, y) for zz in range(4)]
    peers += [(at(xx, z, cc), h, y) for xx, cc in xpeers]
    peers += [(ka, h, up), (ka, h, down)]
    for peer in peers:
        pl.semaphore_signal(barrier, inc=1, device_id=peer, device_id_type=MESH)
    for a in range(3):
        for m in range(CHUNKS):
            own[m][a].start()
    load.start()
    pl.semaphore_wait(barrier, len(peers))

    send_z(0, 0)
    send_z(0, 1)
    product[...] = jnp.zeros_like(product)
    load.wait()
    prepare(gloc, h, range(4))
    send_z(0, 2)
    send_x(0, 0)
    send_z(1, 0)
    send_z(1, 1)
    share_less(0, (1, 2))
    send_x(0, 1)
    send_z(1, 2)
    send_x(0, 2)
    send_z(2, 0)
    send_x(1, 0)
    share_less(1, (1, 2))
    send_z(2, 1)
    transform(0)
    send_x(1, 1)
    send_z(2, 2)
    back_z(0)
    send_x(1, 2)
    send_z(3, 0)
    send_x(2, 0)
    share_less(2, (1, 2))
    send_z(3, 1)
    transform(1)
    send_x(2, 1)
    send_z(3, 2)
    back_z(1)
    send_x(2, 2)
    spread_y(0, 0)
    spread_y(0, 3)
    spread_y(0, 1)
    spread_y(0, 2)
    send_x(3, 0)
    share_less(3, (1, 2))
    share_less(0, (0, 3))
    transform(2)
    send_x(3, 1)
    relay_y(0, 0)
    relay_y(0, 3)
    relay_y(0, 1)
    relay_y(0, 2)
    back_z(2)
    send_x(3, 2)
    share_less(1, (0, 3))
    transform(3)
    spread_y(1, 0)
    spread_y(1, 3)
    spread_y(1, 1)
    spread_y(1, 2)
    wait_near(0)
    wait_y(0)
    multiply(0, h, 0, 2)
    back_z(3)
    spread_y(2, 0)
    relay_y(1, 0)
    relay_y(1, 3)
    spread_y(2, 3)
    relay_y(1, 1)
    relay_y(1, 2)
    spread_y(2, 1)
    spread_y(2, 2)
    spread_y(3, 0)
    relay_y(2, 0)
    relay_y(2, 3)
    spread_y(3, 3)
    relay_y(2, 1)
    spread_y(3, 1)
    share_less(2, (0, 3))
    share_less(3, (0, 3))
    relay_y(2, 2)
    spread_y(3, 2)
    wait_near(1)
    wait_y(1)
    multiply(1, h, 0, 2)
    wait_less(0)
    wait_less(1)
    prepare(grem, 1 - h, range(0, 2))
    multiply(0, 1 - h, 0, 1)
    multiply(1, 1 - h, 0, 1)
    relay_y(3, 0)
    relay_y(3, 3)
    relay_y(3, 1)
    relay_y(3, 2)
    wait_near(2)
    wait_y(2)
    multiply(2, h, 0, 2)
    multiply(2, 1 - h, 0, 1)
    wait_less(2)
    wait_less(3)
    prepare(grem, 1 - h, range(2, 4))
    multiply(0, 1 - h, 1, 2)
    multiply(1, 1 - h, 1, 2)
    multiply(2, 1 - h, 1, 2)
    wait_near(3)
    multiply_one(3, y)
    multiply_one(3, up)
    multiply_one(3, down)
    wait_y(3)
    multiply_one(3, (y + 2) % 4)
    done(zbuf.at[:, :, pl.ds(0, 3)], zs.at[0])
    done(tile.at[:, :, pl.ds(0, 7)], zs.at[1])
    done(zbuf.at[:, 0], zs.at[2])
    done(tile.at[:, 0, pl.ds(0, 7)], zs.at[3])
    done(zbuf.at[:, 0, pl.ds(0, 3)], zs.at[4])
    done(zbuf.at[:, pl.ds(0, 2)], zs.at[5])
    done(zbuf.at[:, 0], zs.at[6])


def body(green_less, green_great, screened):
    dma = pltpu.SemaphoreType.DMA
    block = jax.ShapeDtypeStruct(green_less.shape, jnp.float32)
    f32, bf16 = jnp.float32, jnp.bfloat16
    product = pl.pallas_call(
        kernel,
        out_shape=block,
        in_specs=[pl.BlockSpec(memory_space=pl.ANY)] * 3,
        out_specs=pl.BlockSpec(memory_space=pltpu.VMEM),
        scratch_shapes=[
            pltpu.VMEM((CHUNKS, 3, 4, 2, ZROWS, CCOLS), f32),
            pltpu.VMEM((CHUNKS, 3, 8, 4, 2, TROWS, CCOLS), f32),
            pltpu.VMEM((3, 4, 8, 2, TROWS, CCOLS), f32),
            pltpu.VMEM((4, 8, 2, TROWS, CCOLS), f32),
            pltpu.VMEM((CHUNKS, 8, 4, 2, TROWS, CCOLS), f32),
            pltpu.VMEM((CHUNKS, 4, 2, ZROWS, CCOLS), f32),
            pltpu.VMEM((4, 2, 2, ROWS, CCOLS), f32),
            pltpu.VMEM((2, ROWS, COLS), f32),
            pltpu.VMEM((2, ROWS, COLS), f32),
            pltpu.VMEM((8, 256, 512), bf16),
            pltpu.VMEM((8, 256, 512), bf16),
            dma((4,)), dma((7,)),
            dma((CHUNKS, 3)), dma((CHUNKS, 3)),
            dma((CHUNKS,)), dma((CHUNKS,)), dma((CHUNKS, 3)),
            dma((CHUNKS, 4)), dma((CHUNKS,)), dma((CHUNKS,)),
        ],
        compiler_params=pltpu.CompilerParams(collective_id=0, has_side_effects=True, vmem_limit_bytes=52 << 20),
        name="collide",
    )(green_less, green_great, screened)
    collision = product * NORM
    return collision, green_less + collision


def solution(mesh):
    spec = P(None, "ka", "tr", "tc")
    return jax.shard_map(body, mesh=mesh, in_specs=(spec,) * 3, out_specs=(spec,) * 2, check_vma=False)
```
